512 devices in a mesh: ctx: 32 (over z, core), exp: 16 (over x, y).
Axes of the slice: x: 4, y: 4, z: 16, core: 2. Of those that a mesh axis runs over, the one named last changes fastest.
Arguments:
- scan_input: bfloat16 [4096, 4096], P('ctx', 'exp'), may hold values from -6 to 6
- step_size: bfloat16 [4096, 4096], P('ctx', 'exp'), may hold values from 0.5 to 2
- decay_rate: float32 [16, 4096], P(None, 'exp'), may hold values from 2e-06 to 0.1
- input_proj: float32 [16, 4096], P(None, 'ctx'), may hold values from -1.5 to 1.5
- output_proj: float32 [16, 4096], P(None, 'ctx'), may hold values from -0.4 to 0.4
- skip_gain: float32 [4096], P('exp'), may hold values from 0.5 to 1.5
- block_states: float32 [32, 16, 4096], P('ctx', None, 'exp'), may hold values from -24 to 24
- end_grad: float32 [16, 4096], P(None, 'exp'), may hold values from -6 to 6
- scan_grad: bfloat16 [4096, 4096], P('ctx', 'exp'), may hold values from -6 to 6
- moe_grad: bfloat16 [4096, 4096], P(('ctx', 'exp')), may hold values from -6 to 6
- route: int32 [4096, 2], P(('ctx', 'exp')), may hold values from 0 to 15, all different within a row; in each aligned block of 8 rows (0 to 7, 8 to 15, ...) at most 2 rows name the same one
- gate_prob: float32 [4096, 2], P(('ctx', 'exp')), may hold values from 0.1 to 0.9
- w_down: bfloat16 [16, 7168, 4096], P('exp', 'ctx'), may hold values from -0.0625 to 0.0625
- hidden_saved: bfloat16 [16, 1024, 7168], P('exp', None, 'ctx'), may hold values from -6 to 6
Outputs:
- input_grad: bfloat16 [4096, 4096], P('ctx', 'exp')
- step_grad: bfloat16 [4096, 4096], P('ctx', 'exp')
- in_proj_grad: float32 [16, 4096], P(None, 'ctx')
- out_proj_grad: float32 [16, 4096], P(None, 'ctx')
- decay_grad: float32 [16, 4096], P(None, 'exp')
- down_grad: bfloat16 [16, 7168, 4096], P('exp', 'ctx')
- hidden_grad: bfloat16 [16, 1024, 7168], P('exp', None, 'ctx')
The draws below stay inside these ranges and needn't reach their ends.
Inputs may be any that keep to these rules, and one draw needn't show every extreme that they name: `route`: the experts of one token differ. Within the 8 tokens of one source (aligned blocks of 8 rows) no expert is named more than 2 times, a bound that some block reaches.
All inputs are finite; a program needn't handle non-finite values.
Results may differ from the reference program's by a relative error of at most 0.0049.
Values may be sent and summed in bfloat16 or wider, within the bound.
A program may use at most 64 MiB of HBM per device.

```python
import math
import jax
import jax.numpy as jnp
import numpy as np
from jax import lax

D = 4096
INNER = 4096
NSTATE = 16
FF = 7168
EXPERTS = 16
TOPK = 2
TOK_CTX = 128
TOKENS = 4096
TOK_MOE = 8
CAP = 2
SLOTS = 1024
N_CTX = 32


def shard_levels(rng, extent, split, smallest, high):
    level = 1.0
    for dim, blocks in split:
        heights = jax.random.uniform(jax.random.fold_in(jax.random.fold_in(rng, 6), dim), (blocks,), jnp.float32, smallest / len(split), high / len(split))
        level = level * jnp.repeat(jnp.exp(heights), extent[dim] // blocks).reshape((-1,) + (1,) * (len(extent) - 1 - dim))
    return level


def shared_out(own_key, own, number, rows, number_of, top, most, slope):
    order = jax.random.permutation(own_key, number_of)
    crowded, usual = load_shares(number_of, rows * top, most, slope, True), load_shares(number_of, rows * top, most, slope, False)
    places = jnp.arange(number_of)

    def named(sizes, offset_by):
        used = int((sizes > 0).sum())
        fixed = max(1, used // 4)
        moved = fixed + (places - fixed + offset_by * (used - fixed)) % max(1, number_of - fixed)
        return jnp.zeros((number_of,), jnp.int32).at[order[jnp.where(places < fixed, places, moved)]].set(jnp.asarray(sizes, jnp.int32))

    sizes = jnp.where(number % 4 == 0, named(crowded, number // 4), named(usual, number - number // 4 - 1))
    mixed = jax.random.permutation(jax.random.fold_in(own, 3), number_of)
    giver, taker = mixed[0:number_of // 2 * 2:2], mixed[1:number_of // 2 * 2:2]
    room = jnp.minimum(sizes[giver] - 1, most - sizes[taker]) // 2
    room = jnp.where((giver == order[0]) | (taker == order[0]) | (sizes[taker] == 0), 0, jnp.maximum(room, 0))
    moved = jax.random.randint(jax.random.fold_in(own, 4), (number_of // 2,), 0, 1 << 20) % (room + 1)
    sizes = sizes.at[giver].add(-moved).at[taker].add(moved)
    members = jnp.searchsorted(jnp.cumsum(sizes), jnp.arange(rows * top), side="right").astype(jnp.int32)
    grid = members.reshape(top, rows).T
    grid = grid[jax.random.permutation(jax.random.fold_in(own, 1), rows)]
    offset_by = jax.random.randint(jax.random.fold_in(own, 2), (rows, 1), 0, top)
    return jnp.take_along_axis(grid, (jnp.arange(top)[None, :] + offset_by) % top, axis=1)


def load_shares(number_of, total, most, slope, full):
    weights = [(1 << 20) // math.isqrt(standing ** slope) + 1 for standing in range(1, number_of + 1)]
    largest = most if full else min(most, max(-(-total // number_of), total * weights[0] // sum(weights)))
    least = 1 if total - largest >= number_of - 1 else 0
    given, rest = [largest] + [least] * (number_of - 1), total - largest - least * (number_of - 1)
    while rest > 0:
        candidates = [i for i in range(1, number_of) if given[i] < largest] or [i for i in range(1, number_of) if given[i] < most]
        mass, left = sum([weights[i] for i in candidates]), rest
        for i in candidates:
            more = min(most - given[i], max(1, left * weights[i] // mass), rest)
            given[i] = given[i] + more
            rest = rest - more
    return np.array(given)


def centred(own_key, dims, scale, bound, shards=(), held_as=jnp.bfloat16):
    entries = scale * jax.random.normal(own_key, dims, jnp.float32)
    if shards:
        entries = entries * shard_levels(own_key, dims, shards, -0.22, 0.18)
    return jnp.clip(entries, -bound, bound).astype(held_as)


def setup_inputs(seed: int = 0) -> dict:
    seeds = jax.random.split(jax.random.key(seed), 15)
    scan_input = centred(seeds[0], (TOKENS, INNER), 1.0, 6.0, ((0, 32), (1, 16)))
    step_size = jnp.clip(jnp.exp(math.log(2.0) - 1.3862944 * jax.random.uniform(seeds[1], (TOKENS, INNER), jnp.float32) ** shard_levels(seeds[1], (TOKENS, INNER), ((0, 32), (1, 16)), -0.2, 0.2)), 0.5, 2.0).astype(jnp.bfloat16)
    decay_rate = jnp.clip(jnp.exp(math.log(0.1) - 10.819778 * jax.random.uniform(seeds[2], (NSTATE, INNER), jnp.float32) ** shard_levels(seeds[2], (NSTATE, INNER), ((1, 16),), -0.2, 0.2)), 1.9999999949504854e-06, 0.1)
    input_proj = centred(seeds[3], (NSTATE, TOKENS), 0.25, 1.5, ((1, 32),), jnp.float32)
    output_proj = centred(seeds[4], (NSTATE, TOKENS), 0.0625, 0.4, ((1, 32),), jnp.float32)
    skip_gain = jnp.clip(0.5 + 1.0 * jax.random.uniform(seeds[5], (INNER,), jnp.float32) ** shard_levels(seeds[5], (INNER,), ((0, 16),), -0.2, 0.2), 0.5, 1.5)
    block_states = centred(seeds[6], (N_CTX, NSTATE, INNER), 4.0, 24.0, ((0, 32), (2, 16)), jnp.float32)
    end_grad = centred(seeds[7], (NSTATE, INNER), 1.0, 6.0, ((1, 16),), jnp.float32)
    scan_grad = centred(seeds[8], (TOKENS, INNER), 1.0, 6.0, ((0, 32), (1, 16)))
    moe_grad = centred(seeds[9], (TOKENS, D), 1.0, 6.0, ((0, 512),))
    route_keys = jax.random.split(jax.random.fold_in(seeds[10], 1), TOKENS // TOK_MOE)
    route_turns = jax.random.permutation(jax.random.fold_in(seeds[10], 3), TOKENS // TOK_MOE)
    route = jax.vmap(lambda own, number: shared_out(jax.random.fold_in(seeds[10], 2), own, number, TOK_MOE, EXPERTS, TOPK, CAP, 2))(route_keys, route_turns).reshape((TOKENS, TOPK))
    gate_prob = jnp.clip(0.1 + 0.79999997 * jax.random.uniform(seeds[11], (TOKENS, TOPK), jnp.float32) ** shard_levels(seeds[11], (TOKENS, TOPK), ((0, 512),), -0.2, 0.2), 0.1, 0.9)
    w_down = centred(seeds[12], (EXPERTS, FF, D), FF ** -0.5, 0.0625, ((0, 16), (1, 32)))
    hidden_saved = centred(seeds[13], (EXPERTS, SLOTS, FF), 1.0, 6.0, ((0, 16), (2, 32)))
    return dict(scan_input=scan_input, step_size=step_size, decay_rate=decay_rate, input_proj=input_proj, output_proj=output_proj, skip_gain=skip_gain, block_states=block_states, end_grad=end_grad, scan_grad=scan_grad, moe_grad=moe_grad, route=route, gate_prob=gate_prob, w_down=w_down, hidden_saved=hidden_saved)


def reference(scan_input, step_size, decay_rate, input_proj, output_proj, skip_gain, block_states, end_grad, scan_grad, moe_grad, route, gate_prob, w_down, hidden_saved):
    inputs_all = scan_input.astype(jnp.float32).reshape(N_CTX, TOK_CTX, INNER)
    steps_all = step_size.astype(jnp.float32).reshape(N_CTX, TOK_CTX, INNER)
    grads_all = scan_grad.astype(jnp.float32).reshape(N_CTX, TOK_CTX, INNER)
    in_mats = input_proj.reshape(NSTATE, N_CTX, TOK_CTX).transpose(1, 2, 0)
    out_mats = output_proj.reshape(NSTATE, N_CTX, TOK_CTX).transpose(1, 2, 0)

    def one_block(incoming, blockdata):
        inputs, steps, bmats, cmats, first_state, grads = blockdata
        decays = jnp.exp(-steps[:, None, :] * decay_rate[None])
        driving = (steps * inputs)[:, None, :] * bmats[:, :, None]

        def forward_step(state, element):
            state = element[0] * state + element[1]
            return state, state

        _, states = lax.scan(forward_step, first_state, (decays, driving))
        before = jnp.concatenate([first_state[None], states[:-1]], axis=0)
        sources = cmats[:, :, None] * grads[:, None, :]

        def backward_step(running, element):
            value = element[1] + running
            return element[0] * value, value

        outgoing, adjoint = lax.scan(backward_step, incoming, (decays, sources), reverse=True)
        input_part = steps * jnp.sum(bmats[:, :, None] * adjoint, axis=1) + skip_gain[None] * grads
        step_part = jnp.sum(adjoint * (bmats[:, :, None] * inputs[:, None, :] - decay_rate[None] * decays * before), axis=1)
        in_part = jnp.sum(adjoint * (steps * inputs)[:, None, :], axis=2)
        out_part = jnp.sum(states * grads[:, None, :], axis=2)
        rate_part = jnp.sum(adjoint * (-steps[:, None, :] * decays * before), axis=0)
        return outgoing, (input_part.astype(jnp.bfloat16), step_part.astype(jnp.bfloat16), in_part, out_part, rate_part)

    _, results = lax.scan(one_block, end_grad, (inputs_all, steps_all, in_mats, out_mats, block_states, grads_all), reverse=True)
    input_grad = results[0].reshape(TOKENS, INNER)
    step_grad = results[1].reshape(TOKENS, INNER)
    in_proj_grad = results[2].transpose(2, 0, 1).reshape(NSTATE, TOKENS)
    out_proj_grad = results[3].transpose(2, 0, 1).reshape(NSTATE, TOKENS)
    decay_grad = jnp.sum(results[4], axis=0)

    sources_count = TOKENS // TOK_MOE
    pairs_source = TOK_MOE * TOPK
    weighted = (gate_prob[:, :, None] * moe_grad.astype(jnp.float32)[:, None, :]).astype(jnp.bfloat16)
    weighted = weighted.reshape(TOKENS * TOPK, D)
    experts_of = route.reshape(sources_count, pairs_source)
    onehot = (experts_of[:, :, None] == jnp.arange(EXPERTS, dtype=jnp.int32)[None, None, :]).astype(jnp.int32)
    earlier = jnp.cumsum(onehot, axis=1) - onehot
    ranks = jnp.sum(earlier * onehot, axis=2)
    source_ids = jnp.arange(sources_count, dtype=jnp.int32)[:, None]
    slot_ids = (source_ids * CAP + ranks).reshape(-1).astype(jnp.int32)
    expert_ids = experts_of.reshape(-1).astype(jnp.int32)
    dispatched = jnp.zeros((EXPERTS, SLOTS, D), jnp.bfloat16).at[expert_ids, slot_ids].set(weighted)

    def per_expert(element):
        buffer, weight, saved = element
        weight_part = jnp.dot(saved.T, buffer, preferred_element_type=jnp.float32).astype(jnp.bfloat16)
        saved_part = jnp.dot(buffer, weight.T, preferred_element_type=jnp.float32).astype(jnp.bfloat16)
        return weight_part, saved_part

    down_grad, hidden_grad = lax.map(per_expert, (dispatched, w_down, hidden_saved))
    return (input_grad, step_grad, in_proj_grad, out_proj_grad, decay_grad, down_grad, hidden_grad)
```

```python
import jax
import jax.numpy as jnp
from jax import lax
from jax.sharding import PartitionSpec as P

EXPERTS = 16


def shifted_from(value, axis, distance):
    count = lax.axis_size(axis)
    return lax.ppermute(value, axis, [(source, source - distance) for source in range(distance, count)])


def butterfly_sum(value, axis):
    count = lax.axis_size(axis)
    distance = 1
    while distance < count:
        pairs = [(source, source ^ distance) for source in range(count)]
        value = jax.tree.map(lambda part: part + lax.ppermute(part, axis, pairs), value)
        distance *= 2
    return value


def slot_buffer(moe_grad, route, gate_prob, capacity):
    pair_count = route.shape[0] * route.shape[1]
    weighted = (gate_prob[:, :, None] * moe_grad.astype(jnp.float32)[:, None, :]).astype(
        jnp.bfloat16
    )
    weighted = weighted.reshape(pair_count, moe_grad.shape[1])
    flat_route = route.reshape(pair_count)
    onehot = (flat_route[:, None] == jnp.arange(EXPERTS, dtype=jnp.int32)[None, :]).astype(
        jnp.int32
    )
    ranks = jnp.sum((jnp.cumsum(onehot, axis=0) - onehot) * onehot, axis=1)
    target = flat_route * capacity + ranks
    placing = (target[:, None] == jnp.arange(EXPERTS * capacity, dtype=jnp.int32)[None, :]).astype(
        jnp.bfloat16
    )
    buffer = jnp.einsum("ps,pd->sd", placing, weighted, preferred_element_type=jnp.float32).astype(
        jnp.bfloat16
    )
    return buffer.reshape(EXPERTS, capacity, moe_grad.shape[1])


def body(
    scan_input,
    step_size,
    decay_rate,
    input_proj,
    output_proj,
    skip_gain,
    block_states,
    end_grad,
    scan_grad,
    moe_grad,
    route,
    gate_prob,
    w_down,
    hidden_saved,
):
    inputs = scan_input.astype(jnp.float32)
    steps = step_size.astype(jnp.float32)
    grads = scan_grad.astype(jnp.float32)
    bmats = input_proj.T
    cmats = output_proj.T
    first_state = block_states[0]

    def forward_step(state, element):
        inp, stp, bcol, grad = element
        decay = jnp.exp(-stp[None] * decay_rate)
        fresh = decay * state + (stp * inp)[None] * bcol[:, None]
        return (fresh, (state, jnp.sum(fresh * grad[None], axis=1)))

    _, (before, out_cols) = lax.scan(
        forward_step, first_state, (inputs, steps, bmats, grads), unroll=8
    )

    def seed_step(running, element):
        stp, ccol, grad = element
        decay = jnp.exp(-stp[None] * decay_rate)
        value = ccol[:, None] * grad[None] + running
        return (decay * value, None)

    seed, _ = lax.scan(
        seed_step, jnp.zeros_like(first_state), (steps, cmats, grads), reverse=True, unroll=8
    )
    shrink = jnp.exp(-decay_rate * jnp.sum(steps, axis=0)[None])
    position = lax.axis_index("ctx")
    count = lax.axis_size("ctx")
    is_last = position == count - 1
    pair = jnp.stack(
        [jnp.where(is_last, 0.0, shrink), jnp.where(is_last, shrink * end_grad + seed, seed)]
    )
    distance = 1
    while distance < count:
        later = shifted_from(pair, "ctx", distance)
        present = position + distance < count
        composed = jnp.stack([pair[0] * later[0], pair[0] * later[1] + pair[1]])
        pair = jnp.where(present, composed, pair)
        distance *= 2
    entering = jnp.where(is_last, end_grad, shifted_from(pair[1], "ctx", 1))

    def adjoint_step(carry, element):
        running, rate_acc = carry
        inp, stp, bcol, ccol, grad, prior = element
        decay = jnp.exp(-stp[None] * decay_rate)
        value = ccol[:, None] * grad[None] + running
        input_row = stp * jnp.sum(bcol[:, None] * value, axis=0) + skip_gain * grad
        step_row = jnp.sum(value * (bcol[:, None] * inp[None] - decay_rate * decay * prior), axis=0)
        in_col = jnp.sum(value * (stp * inp)[None], axis=1)
        rate_acc = rate_acc + value * (-stp[None] * decay * prior)
        return (
            (decay * value, rate_acc),
            (input_row.astype(jnp.bfloat16), step_row.astype(jnp.bfloat16), in_col),
        )

    (_, rate_local), (input_grad, step_grad, in_cols) = lax.scan(
        adjoint_step,
        (entering, jnp.zeros_like(entering)),
        (inputs, steps, bmats, cmats, grads, before),
        reverse=True,
        unroll=8,
    )
    in_proj_grad, out_proj_grad = butterfly_sum((in_cols.T, out_cols.T), "exp")
    decay_grad = butterfly_sum(rate_local, "ctx")
    slot_total = hidden_saved.shape[1]
    capacity = slot_total // (lax.axis_size("ctx") * lax.axis_size("exp"))
    buffer = slot_buffer(moe_grad, route, gate_prob, capacity)
    received_rows = lax.all_to_all(buffer, "exp", split_axis=0, concat_axis=1, tiled=True)
    all_rows = lax.all_gather(received_rows, "ctx", axis=1, tiled=True)
    weight_total = jnp.einsum(
        "lrf,lrd->lfd", hidden_saved, all_rows, preferred_element_type=jnp.float32
    )
    hidden_grad = jnp.einsum(
        "lrd,lfd->lrf", all_rows, w_down, preferred_element_type=jnp.float32
    ).astype(jnp.bfloat16)
    down_grad = weight_total.astype(jnp.bfloat16)
    return (input_grad, step_grad, in_proj_grad, out_proj_grad, decay_grad, down_grad, hidden_grad)


def solution(mesh):
    placed = (
        P("ctx", "exp"),
        P("ctx", "exp"),
        P(None, "exp"),
        P(None, "ctx"),
        P(None, "ctx"),
        P("exp"),
        P("ctx", None, "exp"),
        P(None, "exp"),
        P("ctx", "exp"),
        P(("ctx", "exp"), None),
        P(("ctx", "exp"), None),
        P(("ctx", "exp"), None),
        P("exp", "ctx", None),
        P("exp", None, "ctx"),
    )
    return jax.shard_map(
        body,
        mesh=mesh,
        in_specs=placed,
        out_specs=(
            P("ctx", "exp"),
            P("ctx", "exp"),
            P(None, "ctx"),
            P(None, "ctx"),
            P(None, "exp"),
            P("exp", "ctx", None),
            P("exp", None, "ctx"),
        ),
        check_vma=False,
    )
```

```python
import jax
import jax.numpy as jnp
from jax import lax
from jax.experimental import pallas as pl
from jax.experimental.pallas import tpu as pltpu
from jax.sharding import PartitionSpec as P

EXPERTS = 16


def shifted_from(value, axis, distance):
    count = lax.axis_size(axis)
    return lax.ppermute(value, axis, [(source, source - distance) for source in range(distance, count)])


def butterfly_sum(value, axis):
    count = lax.axis_size(axis)
    distance = 1
    while distance < count:
        pairs = [(source, source ^ distance) for source in range(count)]
        value = jax.tree.map(lambda part: part + lax.ppermute(part, axis, pairs), value)
        distance *= 2
    return value


def local_scans_kernel(decay_ref, drive_ref, source_ref, first_ref, states_ref, seed_ref):
    count = decay_ref.shape[0]

    def forward(t, state):
        state = decay_ref[t] * state + drive_ref[t]
        states_ref[t] = state
        return state

    lax.fori_loop(0, count, forward, first_ref[...], unroll=8)

    def backward(i, running):
        t = count - 1 - i
        return decay_ref[t] * (source_ref[t] + running)

    seed_ref[...] = lax.fori_loop(0, count, backward, jnp.zeros_like(first_ref[...]), unroll=8)


def local_scans(decays, driving, sources, first_state):
    return pl.pallas_call(
        local_scans_kernel,
        out_shape=(
            jax.ShapeDtypeStruct(decays.shape, jnp.float32),
            jax.ShapeDtypeStruct(first_state.shape, jnp.float32),
        ),
        cost_estimate=pl.CostEstimate(
            flops=4 * decays.size, bytes_accessed=16 * decays.size, transcendentals=0
        ),
    )(decays, driving, sources, first_state)


def adjoint_scan_kernel(decay_ref, source_ref, entering_ref, adjoint_ref):
    count = decay_ref.shape[0]

    def backward(i, running):
        t = count - 1 - i
        value = source_ref[t] + running
        adjoint_ref[t] = value
        return decay_ref[t] * value

    lax.fori_loop(0, count, backward, entering_ref[...], unroll=8)


def adjoint_scan(decays, sources, entering):
    return pl.pallas_call(
        adjoint_scan_kernel,
        out_shape=jax.ShapeDtypeStruct(decays.shape, jnp.float32),
        cost_estimate=pl.CostEstimate(
            flops=2 * decays.size, bytes_accessed=12 * decays.size, transcendentals=0
        ),
    )(decays, sources, entering)


def slot_buffer(moe_grad, route, gate_prob, capacity):
    pair_count = route.shape[0] * route.shape[1]
    weighted = (gate_prob[:, :, None] * moe_grad.astype(jnp.float32)[:, None, :]).astype(
        jnp.bfloat16
    )
    weighted = weighted.reshape(pair_count, moe_grad.shape[1])
    flat_route = route.reshape(pair_count)
    onehot = (flat_route[:, None] == jnp.arange(EXPERTS, dtype=jnp.int32)[None, :]).astype(
        jnp.int32
    )
    ranks = jnp.sum((jnp.cumsum(onehot, axis=0) - onehot) * onehot, axis=1)
    target = flat_route * capacity + ranks
    placing = (target[:, None] == jnp.arange(EXPERTS * capacity, dtype=jnp.int32)[None, :]).astype(
        jnp.bfloat16
    )
    buffer = jnp.einsum("ps,pd->sd", placing, weighted, preferred_element_type=jnp.float32).astype(
        jnp.bfloat16
    )
    return buffer.reshape(EXPERTS, capacity, moe_grad.shape[1])


def body(
    scan_input,
    step_size,
    decay_rate,
    input_proj,
    output_proj,
    skip_gain,
    block_states,
    end_grad,
    scan_grad,
    moe_grad,
    route,
    gate_prob,
    w_down,
    hidden_saved,
):
    inputs = scan_input.astype(jnp.float32)
    steps = step_size.astype(jnp.float32)
    grads = scan_grad.astype(jnp.float32)
    bmats = input_proj.T
    cmats = output_proj.T
    first_state = block_states[0]
    decays = jnp.exp(-steps[:, None, :] * decay_rate[None])
    driving = (steps * inputs)[:, None, :] * bmats[:, :, None]
    sources = cmats[:, :, None] * grads[:, None, :]
    states, seed = local_scans(decays, driving, sources, first_state)
    before = jnp.concatenate([first_state[None], states[:-1]], axis=0)
    out_cols = jnp.sum(states * grads[:, None, :], axis=2)
    shrink = jnp.exp(-decay_rate * jnp.sum(steps, axis=0)[None])
    position = lax.axis_index("ctx")
    count = lax.axis_size("ctx")
    is_last = position == count - 1
    pair = jnp.stack(
        [jnp.where(is_last, 0.0, shrink), jnp.where(is_last, shrink * end_grad + seed, seed)]
    )
    distance = 1
    while distance < count:
        later = shifted_from(pair, "ctx", distance)
        present = position + distance < count
        composed = jnp.stack([pair[0] * later[0], pair[0] * later[1] + pair[1]])
        pair = jnp.where(present, composed, pair)
        distance *= 2
    entering = jnp.where(is_last, end_grad, shifted_from(pair[1], "ctx", 1))
    adjoint = adjoint_scan(decays, sources, entering)
    input_grad = (
        steps * jnp.sum(bmats[:, :, None] * adjoint, axis=1) + skip_gain[None] * grads
    ).astype(jnp.bfloat16)
    step_grad = jnp.sum(
        adjoint * (bmats[:, :, None] * inputs[:, None, :] - decay_rate[None] * decays * before),
        axis=1,
    ).astype(jnp.bfloat16)
    in_cols = jnp.sum(adjoint * (steps * inputs)[:, None, :], axis=2)
    rate_local = jnp.sum(adjoint * (-steps[:, None, :] * decays * before), axis=0)
    in_proj_grad, out_proj_grad = butterfly_sum((in_cols.T, out_cols.T), "exp")
    decay_grad = butterfly_sum(rate_local, "ctx")
    slot_total = hidden_saved.shape[1]
    capacity = slot_total // (lax.axis_size("ctx") * lax.axis_size("exp"))
    buffer = slot_buffer(moe_grad, route, gate_prob, capacity)
    received_rows = lax.all_to_all(buffer, "exp", split_axis=0, concat_axis=1, tiled=True)
    all_rows = lax.all_gather(received_rows, "ctx", axis=1, tiled=True)
    weight_total = jnp.einsum(
        "lrf,lrd->lfd", hidden_saved, all_rows, preferred_element_type=jnp.float32
    )
    hidden_grad = jnp.einsum(
        "lrd,lfd->lrf", all_rows, w_down, preferred_element_type=jnp.float32
    ).astype(jnp.bfloat16)
    down_grad = weight_total.astype(jnp.bfloat16)
    return (input_grad, step_grad, in_proj_grad, out_proj_grad, decay_grad, down_grad, hidden_grad)


def solution(mesh):
    placed = (
        P("ctx", "exp"),
        P("ctx", "exp"),
        P(None, "exp"),
        P(None, "ctx"),
        P(None, "ctx"),
        P("exp"),
        P("ctx", None, "exp"),
        P(None, "exp"),
        P("ctx", "exp"),
        P(("ctx", "exp"), None),
        P(("ctx", "exp"), None),
        P(("ctx", "exp"), None),
        P("exp", "ctx", None),
        P("exp", None, "ctx"),
    )
    return jax.shard_map(
        body,
        mesh=mesh,
        in_specs=placed,
        out_specs=(
            P("ctx", "exp"),
            P("ctx", "exp"),
            P(None, "ctx"),
            P(None, "ctx"),
            P(None, "exp"),
            P("exp", "ctx", None),
            P("exp", None, "ctx"),
        ),
        check_vma=False,
    )
```

```python
import functools

import jax
import jax.numpy as jnp
from jax import lax
from jax.experimental import pallas as pl
from jax.experimental.pallas import tpu as pltpu
from jax.sharding import PartitionSpec as P

EXPERTS = 16


def shifted_from(value, axis, distance):
    count = lax.axis_size(axis)
    return lax.ppermute(value, axis, [(source, source - distance) for source in range(distance, count)])


def local_scans_kernel(decay_ref, drive_ref, source_ref, first_ref, states_ref, seed_ref):
    count = decay_ref.shape[0]

    def forward(t, state):
        state = decay_ref[t] * state + drive_ref[t]
        states_ref[t] = state
        return state

    lax.fori_loop(0, count, forward, first_ref[...], unroll=8)

    def backward(i, running):
        t = count - 1 - i
        return decay_ref[t] * (source_ref[t] + running)

    seed_ref[...] = lax.fori_loop(0, count, backward, jnp.zeros_like(first_ref[...]), unroll=8)


def local_scans(decays, driving, sources, first_state):
    return pl.pallas_call(
        local_scans_kernel,
        out_shape=(
            jax.ShapeDtypeStruct(decays.shape, jnp.float32),
            jax.ShapeDtypeStruct(first_state.shape, jnp.float32),
        ),
        cost_estimate=pl.CostEstimate(
            flops=4 * decays.size, bytes_accessed=16 * decays.size, transcendentals=0
        ),
    )(decays, driving, sources, first_state)


def adjoint_scan_kernel(decay_ref, source_ref, entering_ref, adjoint_ref):
    count = decay_ref.shape[0]

    def backward(i, running):
        t = count - 1 - i
        value = source_ref[t] + running
        adjoint_ref[t] = value
        return decay_ref[t] * value

    lax.fori_loop(0, count, backward, entering_ref[...], unroll=8)


def adjoint_scan(decays, sources, entering):
    return pl.pallas_call(
        adjoint_scan_kernel,
        out_shape=jax.ShapeDtypeStruct(decays.shape, jnp.float32),
        cost_estimate=pl.CostEstimate(
            flops=2 * decays.size, bytes_accessed=12 * decays.size, transcendentals=0
        ),
    )(decays, sources, entering)


def exchange_kernel(axis, count, same, x_ref, out_ref, land, send_sems, recv_sems):
    me = lax.axis_index(axis)
    barrier = pltpu.get_barrier_semaphore()
    for k in range(1, count):
        pl.semaphore_signal(
            barrier,
            1,
            device_id={axis: lax.rem(me + k, count)},
            device_id_type=pl.DeviceIdType.MESH,
        )
    pl.semaphore_wait(barrier, count - 1)
    copies = []
    for k in range(1, count):
        peer = lax.rem(me + k, count)
        copy = pltpu.make_async_remote_copy(
            src_ref=x_ref if same else x_ref.at[peer],
            dst_ref=land.at[me],
            send_sem=send_sems.at[k],
            recv_sem=recv_sems.at[k],
            device_id={axis: peer},
            device_id_type=pl.DeviceIdType.MESH,
        )
        copy.start()
        copies.append(copy)
    land[me] = x_ref[...] if same else x_ref[me]
    for copy in copies:
        copy.wait()
    out_ref[...] = land[...]


def exchange(x, axis, same, collective_id):
    count = lax.axis_size(axis)
    block = x.shape if same else x.shape[1:]
    return pl.pallas_call(
        functools.partial(exchange_kernel, axis, count, same),
        out_shape=jax.ShapeDtypeStruct((count,) + block, x.dtype),
        scratch_shapes=[
            pltpu.VMEM((count,) + block, x.dtype),
            pltpu.SemaphoreType.DMA((count,)),
            pltpu.SemaphoreType.DMA((count,)),
        ],
        compiler_params=pltpu.CompilerParams(collective_id=collective_id, has_side_effects=True),
    )(x)


def slot_buffer(moe_grad, route, gate_prob, capacity):
    pair_count = route.shape[0] * route.shape[1]
    weighted = (gate_prob[:, :, None] * moe_grad.astype(jnp.float32)[:, None, :]).astype(
        jnp.bfloat16
    )
    weighted = weighted.reshape(pair_count, moe_grad.shape[1])
    flat_route = route.reshape(pair_count)
    onehot = (flat_route[:, None] == jnp.arange(EXPERTS, dtype=jnp.int32)[None, :]).astype(
        jnp.int32
    )
    ranks = jnp.sum((jnp.cumsum(onehot, axis=0) - onehot) * onehot, axis=1)
    target = flat_route * capacity + ranks
    placing = (target[:, None] == jnp.arange(EXPERTS * capacity, dtype=jnp.int32)[None, :]).astype(
        jnp.bfloat16
    )
    buffer = jnp.einsum("ps,pd->sd", placing, weighted, preferred_element_type=jnp.float32).astype(
        jnp.bfloat16
    )
    return buffer.reshape(EXPERTS, capacity, moe_grad.shape[1])


def body(
    scan_input,
    step_size,
    decay_rate,
    input_proj,
    output_proj,
    skip_gain,
    block_states,
    end_grad,
    scan_grad,
    moe_grad,
    route,
    gate_prob,
    w_down,
    hidden_saved,
):
    inputs = scan_input.astype(jnp.float32)
    steps = step_size.astype(jnp.float32)
    grads = scan_grad.astype(jnp.float32)
    bmats = input_proj.T
    cmats = output_proj.T
    first_state = block_states[0]
    decays = jnp.exp(-steps[:, None, :] * decay_rate[None])
    driving = (steps * inputs)[:, None, :] * bmats[:, :, None]
    sources = cmats[:, :, None] * grads[:, None, :]
    states, seed = local_scans(decays, driving, sources, first_state)
    before = jnp.concatenate([first_state[None], states[:-1]], axis=0)
    out_cols = jnp.sum(states * grads[:, None, :], axis=2)
    shrink = jnp.exp(-decay_rate * jnp.sum(steps, axis=0)[None])
    position = lax.axis_index("ctx")
    count = lax.axis_size("ctx")
    is_last = position == count - 1
    pair = jnp.stack(
        [jnp.where(is_last, 0.0, shrink), jnp.where(is_last, shrink * end_grad + seed, seed)]
    )
    distance = 1
    while distance < count:
        later = shifted_from(pair, "ctx", distance)
        present = position + distance < count
        composed = jnp.stack([pair[0] * later[0], pair[0] * later[1] + pair[1]])
        pair = jnp.where(present, composed, pair)
        distance *= 2
    entering = jnp.where(is_last, end_grad, shifted_from(pair[1], "ctx", 1))
    adjoint = adjoint_scan(decays, sources, entering)
    input_grad = (
        steps * jnp.sum(bmats[:, :, None] * adjoint, axis=1) + skip_gain[None] * grads
    ).astype(jnp.bfloat16)
    step_grad = jnp.sum(
        adjoint * (bmats[:, :, None] * inputs[:, None, :] - decay_rate[None] * decays * before),
        axis=1,
    ).astype(jnp.bfloat16)
    in_cols = jnp.sum(adjoint * (steps * inputs)[:, None, :], axis=2)
    rate_local = jnp.sum(adjoint * (-steps[:, None, :] * decays * before), axis=0)
    col_sums = jnp.sum(exchange(jnp.stack([in_cols.T, out_cols.T]), "exp", True, 1), axis=0)
    in_proj_grad, out_proj_grad = col_sums[0], col_sums[1]
    ctx_count = lax.axis_size("ctx")
    rate_parts = rate_local.reshape(ctx_count, 1, rate_local.size // ctx_count)
    rate_chunk = jnp.sum(exchange(rate_parts, "ctx", False, 2), axis=0)
    decay_grad = exchange(rate_chunk, "ctx", True, 3).reshape(rate_local.shape)
    slot_total = hidden_saved.shape[1]
    capacity = slot_total // (lax.axis_size("ctx") * lax.axis_size("exp"))
    buffer = slot_buffer(moe_grad, route, gate_prob, capacity)
    received_rows = lax.all_to_all(buffer, "exp", split_axis=0, concat_axis=1, tiled=True)
    all_rows = lax.all_gather(received_rows, "ctx", axis=1, tiled=True)
    weight_total = jnp.einsum(
        "lrf,lrd->lfd", hidden_saved, all_rows, preferred_element_type=jnp.float32
    )
    hidden_grad = jnp.einsum(
        "lrd,lfd->lrf", all_rows, w_down, preferred_element_type=jnp.float32
    ).astype(jnp.bfloat16)
    down_grad = weight_total.astype(jnp.bfloat16)
    return (input_grad, step_grad, in_proj_grad, out_proj_grad, decay_grad, down_grad, hidden_grad)


def solution(mesh):
    placed = (
        P("ctx", "exp"),
        P("ctx", "exp"),
        P(None, "exp"),
        P(None, "ctx"),
        P(None, "ctx"),
        P("exp"),
        P("ctx", None, "exp"),
        P(None, "exp"),
        P("ctx", "exp"),
        P(("ctx", "exp"), None),
        P(("ctx", "exp"), None),
        P(("ctx", "exp"), None),
        P("exp", "ctx", None),
        P("exp", None, "ctx"),
    )
    return jax.shard_map(
        body,
        mesh=mesh,
        in_specs=placed,
        out_specs=(
            P("ctx", "exp"),
            P("ctx", "exp"),
            P(None, "ctx"),
            P(None, "ctx"),
            P(None, "exp"),
            P("exp", "ctx", None),
            P("exp", None, "ctx"),
        ),
        check_vma=False,
    )
```

```python
import functools

import jax
import jax.numpy as jnp
from jax import lax
from jax.experimental import pallas as pl
from jax.experimental.pallas import tpu as pltpu
from jax.sharding import PartitionSpec as P

EXPERTS = 16


def local_scans_kernel(decay_ref, drive_ref, source_ref, first_ref, states_ref, seed_ref):
    count = decay_ref.shape[0]

    def forward(t, state):
        state = decay_ref[t] * state + drive_ref[t]
        states_ref[t] = state
        return state

    lax.fori_loop(0, count, forward, first_ref[...], unroll=8)

    def backward(i, running):
        t = count - 1 - i
        return decay_ref[t] * (source_ref[t] + running)

    seed_ref[...] = lax.fori_loop(0, count, backward, jnp.zeros_like(first_ref[...]), unroll=8)


def local_scans(decays, driving, sources, first_state):
    return pl.pallas_call(
        local_scans_kernel,
        out_shape=(
            jax.ShapeDtypeStruct(decays.shape, jnp.float32),
            jax.ShapeDtypeStruct(first_state.shape, jnp.float32),
        ),
        cost_estimate=pl.CostEstimate(
            flops=4 * decays.size, bytes_accessed=16 * decays.size, transcendentals=0
        ),
    )(decays, driving, sources, first_state)


def adjoint_scan_kernel(decay_ref, source_ref, entering_ref, adjoint_ref):
    count = decay_ref.shape[0]

    def backward(i, running):
        t = count - 1 - i
        value = source_ref[t] + running
        adjoint_ref[t] = value
        return decay_ref[t] * value

    lax.fori_loop(0, count, backward, entering_ref[...], unroll=8)


def adjoint_scan(decays, sources, entering):
    return pl.pallas_call(
        adjoint_scan_kernel,
        out_shape=jax.ShapeDtypeStruct(decays.shape, jnp.float32),
        cost_estimate=pl.CostEstimate(
            flops=2 * decays.size, bytes_accessed=12 * decays.size, transcendentals=0
        ),
    )(decays, sources, entering)


def exchange_kernel(axis, count, same, x_ref, out_ref, land, send_sems, recv_sems):
    me = lax.axis_index(axis)
    barrier = pltpu.get_barrier_semaphore()
    for k in range(1, count):
        pl.semaphore_signal(
            barrier,
            1,
            device_id={axis: lax.rem(me + k, count)},
            device_id_type=pl.DeviceIdType.MESH,
        )
    pl.semaphore_wait(barrier, count - 1)
    copies = []
    for k in range(1, count):
        peer = lax.rem(me + k, count)
        copy = pltpu.make_async_remote_copy(
            src_ref=x_ref if same else x_ref.at[peer],
            dst_ref=land.at[me],
            send_sem=send_sems.at[k],
            recv_sem=recv_sems.at[k],
            device_id={axis: peer},
            device_id_type=pl.DeviceIdType.MESH,
        )
        copy.start()
        copies.append(copy)
    land[me] = x_ref[...] if same else x_ref[me]
    for copy in copies:
        copy.wait()
    out_ref[...] = land[...]


def exchange(x, axis, same, collective_id):
    count = lax.axis_size(axis)
    block = x.shape if same else x.shape[1:]
    return pl.pallas_call(
        functools.partial(exchange_kernel, axis, count, same),
        out_shape=jax.ShapeDtypeStruct((count,) + block, x.dtype),
        scratch_shapes=[
            pltpu.VMEM((count,) + block, x.dtype),
            pltpu.SemaphoreType.DMA((count,)),
            pltpu.SemaphoreType.DMA((count,)),
        ],
        compiler_params=pltpu.CompilerParams(collective_id=collective_id, has_side_effects=True),
    )(x)


def relay_kernel(axis, count, x_ref, out_ref, land, send_sems, recv_sems):
    me = lax.axis_index(axis)
    land[...] = jnp.zeros_like(land)
    barrier = pltpu.get_barrier_semaphore()
    for k in range(1, count):
        pl.semaphore_signal(
            barrier,
            1,
            device_id={axis: lax.rem(me + k, count)},
            device_id_type=pl.DeviceIdType.MESH,
        )
    pl.semaphore_wait(barrier, count - 1)
    copies = []
    for k in range(1, count):
        copy = pltpu.make_async_remote_copy(
            src_ref=x_ref,
            dst_ref=land.at[me],
            send_sem=send_sems.at[k],
            recv_sem=recv_sems.at[k],
            device_id={axis: lax.rem(me - k + count, count)},
            device_id_type=pl.DeviceIdType.MESH,
        )
        copies.append(copy)

        @pl.when(me >= k)
        def _():
            copy.start()

    land[me] = x_ref[...]
    for k, copy in enumerate(copies, start=1):

        @pl.when(me >= k)
        def _():
            copy.wait_send()

        @pl.when(me + k < count)
        def _():
            copy.wait_recv()

    out_ref[...] = land[...]


def relay_exchange(x, axis, collective_id):
    count = lax.axis_size(axis)
    return pl.pallas_call(
        functools.partial(relay_kernel, axis, count),
        out_shape=jax.ShapeDtypeStruct((count,) + x.shape, x.dtype),
        scratch_shapes=[
            pltpu.VMEM((count,) + x.shape, x.dtype),
            pltpu.SemaphoreType.DMA((count,)),
            pltpu.SemaphoreType.DMA((count,)),
        ],
        compiler_params=pltpu.CompilerParams(collective_id=collective_id, has_side_effects=True),
    )(x)


def slot_buffer(moe_grad, route, gate_prob, capacity):
    pair_count = route.shape[0] * route.shape[1]
    weighted = (gate_prob[:, :, None] * moe_grad.astype(jnp.float32)[:, None, :]).astype(
        jnp.bfloat16
    )
    weighted = weighted.reshape(pair_count, moe_grad.shape[1])
    flat_route = route.reshape(pair_count)
    onehot = (flat_route[:, None] == jnp.arange(EXPERTS, dtype=jnp.int32)[None, :]).astype(
        jnp.int32
    )
    ranks = jnp.sum((jnp.cumsum(onehot, axis=0) - onehot) * onehot, axis=1)
    target = flat_route * capacity + ranks
    placing = (target[:, None] == jnp.arange(EXPERTS * capacity, dtype=jnp.int32)[None, :]).astype(
        jnp.bfloat16
    )
    buffer = jnp.einsum("ps,pd->sd", placing, weighted, preferred_element_type=jnp.float32).astype(
        jnp.bfloat16
    )
    return buffer.reshape(EXPERTS, capacity, moe_grad.shape[1])


def body(
    scan_input,
    step_size,
    decay_rate,
    input_proj,
    output_proj,
    skip_gain,
    block_states,
    end_grad,
    scan_grad,
    moe_grad,
    route,
    gate_prob,
    w_down,
    hidden_saved,
):
    inputs = scan_input.astype(jnp.float32)
    steps = step_size.astype(jnp.float32)
    grads = scan_grad.astype(jnp.float32)
    bmats = input_proj.T
    cmats = output_proj.T
    first_state = block_states[0]
    decays = jnp.exp(-steps[:, None, :] * decay_rate[None])
    driving = (steps * inputs)[:, None, :] * bmats[:, :, None]
    sources = cmats[:, :, None] * grads[:, None, :]
    states, seed = local_scans(decays, driving, sources, first_state)
    before = jnp.concatenate([first_state[None], states[:-1]], axis=0)
    out_cols = jnp.sum(states * grads[:, None, :], axis=2)
    step_totals = jnp.sum(steps, axis=0)
    shrink = jnp.exp(-decay_rate * step_totals[None])
    position = lax.axis_index("ctx")
    count = lax.axis_size("ctx")
    is_last = position == count - 1
    outgoing = jnp.where(is_last, shrink * end_grad + seed, seed)
    gathered = relay_exchange(
        jnp.concatenate([outgoing, step_totals[None]], axis=0), "ctx", 4
    )
    running = gathered[count - 1, :-1]
    for later in range(count - 2, 0, -1):
        block_shrink = jnp.exp(-decay_rate * gathered[later, -1][None])
        composed = block_shrink * running + gathered[later, :-1]
        running = jnp.where(later > position, composed, running)
    entering = jnp.where(is_last, end_grad, running)
    adjoint = adjoint_scan(decays, sources, entering)
    input_grad = (
        steps * jnp.sum(bmats[:, :, None] * adjoint, axis=1) + skip_gain[None] * grads
    ).astype(jnp.bfloat16)
    step_grad = jnp.sum(
        adjoint * (bmats[:, :, None] * inputs[:, None, :] - decay_rate[None] * decays * before),
        axis=1,
    ).astype(jnp.bfloat16)
    in_cols = jnp.sum(adjoint * (steps * inputs)[:, None, :], axis=2)
    rate_local = jnp.sum(adjoint * (-steps[:, None, :] * decays * before), axis=0)
    col_sums = jnp.sum(exchange(jnp.stack([in_cols.T, out_cols.T]), "exp", True, 1), axis=0)
    in_proj_grad, out_proj_grad = col_sums[0], col_sums[1]
    ctx_count = lax.axis_size("ctx")
    rate_parts = rate_local.reshape(ctx_count, 1, rate_local.size // ctx_count)
    rate_chunk = jnp.sum(exchange(rate_parts, "ctx", False, 2), axis=0)
    decay_grad = exchange(rate_chunk, "ctx", True, 3).reshape(rate_local.shape)
    slot_total = hidden_saved.shape[1]
    capacity = slot_total // (lax.axis_size("ctx") * lax.axis_size("exp"))
    buffer = slot_buffer(moe_grad, route, gate_prob, capacity)
    received_rows = lax.all_to_all(buffer, "exp", split_axis=0, concat_axis=1, tiled=True)
    all_rows = lax.all_gather(received_rows, "ctx", axis=1, tiled=True)
    weight_total = jnp.einsum(
        "lrf,lrd->lfd", hidden_saved, all_rows, preferred_element_type=jnp.float32
    )
    hidden_grad = jnp.einsum(
        "lrd,lfd->lrf", all_rows, w_down, preferred_element_type=jnp.float32
    ).astype(jnp.bfloat16)
    down_grad = weight_total.astype(jnp.bfloat16)
    return (input_grad, step_grad, in_proj_grad, out_proj_grad, decay_grad, down_grad, hidden_grad)


def solution(mesh):
    placed = (
        P("ctx", "exp"),
        P("ctx", "exp"),
        P(None, "exp"),
        P(None, "ctx"),
        P(None, "ctx"),
        P("exp"),
        P("ctx", None, "exp"),
        P(None, "exp"),
        P("ctx", "exp"),
        P(("ctx", "exp"), None),
        P(("ctx", "exp"), None),
        P(("ctx", "exp"), None),
        P("exp", "ctx", None),
        P("exp", None, "ctx"),
    )
    return jax.shard_map(
        body,
        mesh=mesh,
        in_specs=placed,
        out_specs=(
            P("ctx", "exp"),
            P("ctx", "exp"),
            P(None, "ctx"),
            P(None, "ctx"),
            P(None, "exp"),
            P("exp", "ctx", None),
            P("exp", None, "ctx"),
        ),
        check_vma=False,
    )
```

```python
import functools
import math

import jax
import jax.numpy as jnp
from jax import lax
from jax.experimental import pallas as pl
from jax.experimental.pallas import tpu as pltpu
from jax.sharding import PartitionSpec as P

EXPERTS = 16


CTX = ("z", "core")


def axis_count(axes):
    return math.prod(lax.axis_size(name) for name in axes)


def axis_position(axes):
    flat = 0
    for name in axes:
        flat = flat * lax.axis_size(name) + lax.axis_index(name)
    return flat


def device_at(axes, flat):
    place = {}
    for name in reversed(axes):
        size = lax.axis_size(name)
        place[name] = lax.rem(flat, size)
        flat = flat // size
    return place


def shifted_from(value, axis, distance):
    count = axis_count(axis)
    return lax.ppermute(value, axis, [(source, source - distance) for source in range(distance, count)])


def local_scans_kernel(decay_ref, drive_ref, source_ref, first_ref, states_ref, seed_ref):
    count = decay_ref.shape[0]

    def forward(t, state):
        state = decay_ref[t] * state + drive_ref[t]
        states_ref[t] = state
        return state

    lax.fori_loop(0, count, forward, first_ref[...], unroll=8)

    def backward(i, running):
        t = count - 1 - i
        return decay_ref[t] * (source_ref[t] + running)

    seed_ref[...] = lax.fori_loop(0, count, backward, jnp.zeros_like(first_ref[...]), unroll=8)


def local_scans(decays, driving, sources, first_state):
    return pl.pallas_call(
        local_scans_kernel,
        out_shape=(
            jax.ShapeDtypeStruct(decays.shape, jnp.float32),
            jax.ShapeDtypeStruct(first_state.shape, jnp.float32),
        ),
        cost_estimate=pl.CostEstimate(
            flops=4 * decays.size, bytes_accessed=16 * decays.size, transcendentals=0
        ),
    )(decays, driving, sources, first_state)


def adjoint_scan_kernel(decay_ref, source_ref, entering_ref, adjoint_ref):
    count = decay_ref.shape[0]

    def backward(i, running):
        t = count - 1 - i
        value = source_ref[t] + running
        adjoint_ref[t] = value
        return decay_ref[t] * value

    lax.fori_loop(0, count, backward, entering_ref[...], unroll=8)


def adjoint_scan(decays, sources, entering):
    return pl.pallas_call(
        adjoint_scan_kernel,
        out_shape=jax.ShapeDtypeStruct(decays.shape, jnp.float32),
        cost_estimate=pl.CostEstimate(
            flops=2 * decays.size, bytes_accessed=12 * decays.size, transcendentals=0
        ),
    )(decays, sources, entering)


def exchange_kernel(axis, count, same, x_ref, out_ref, land, send_sems, recv_sems):
    me = axis_position(axis)
    barrier = pltpu.get_barrier_semaphore()
    for k in range(1, count):
        pl.semaphore_signal(
            barrier,
            1,
            device_id=device_at(axis, lax.rem(me + k, count)),
            device_id_type=pl.DeviceIdType.MESH,
        )
    pl.semaphore_wait(barrier, count - 1)
    copies = []
    for k in range(1, count):
        peer = lax.rem(me + k, count)
        copy = pltpu.make_async_remote_copy(
            src_ref=x_ref if same else x_ref.at[peer],
            dst_ref=land.at[me],
            send_sem=send_sems.at[k],
            recv_sem=recv_sems.at[k],
            device_id=device_at(axis, peer),
            device_id_type=pl.DeviceIdType.MESH,
        )
        copy.start()
        copies.append(copy)
    land[me] = x_ref[...] if same else x_ref[me]
    for copy in copies:
        copy.wait()
    out_ref[...] = land[...]


def exchange(x, axis, same, collective_id):
    count = axis_count(axis)
    block = x.shape if same else x.shape[1:]
    return pl.pallas_call(
        functools.partial(exchange_kernel, axis, count, same),
        out_shape=jax.ShapeDtypeStruct((count,) + block, x.dtype),
        scratch_shapes=[
            pltpu.VMEM((count,) + block, x.dtype),
            pltpu.SemaphoreType.DMA((count,)),
            pltpu.SemaphoreType.DMA((count,)),
        ],
        compiler_params=pltpu.CompilerParams(collective_id=collective_id, has_side_effects=True),
    )(x)


def slot_buffer(moe_grad, route, gate_prob, capacity):
    pair_count = route.shape[0] * route.shape[1]
    weighted = (gate_prob[:, :, None] * moe_grad.astype(jnp.float32)[:, None, :]).astype(
        jnp.bfloat16
    )
    weighted = weighted.reshape(pair_count, moe_grad.shape[1])
    flat_route = route.reshape(pair_count)
    onehot = (flat_route[:, None] == jnp.arange(EXPERTS, dtype=jnp.int32)[None, :]).astype(
        jnp.int32
    )
    ranks = jnp.sum((jnp.cumsum(onehot, axis=0) - onehot) * onehot, axis=1)
    target = flat_route * capacity + ranks
    placing = (target[:, None] == jnp.arange(EXPERTS * capacity, dtype=jnp.int32)[None, :]).astype(
        jnp.bfloat16
    )
    buffer = jnp.einsum("ps,pd->sd", placing, weighted, preferred_element_type=jnp.float32).astype(
        jnp.bfloat16
    )
    return buffer.reshape(EXPERTS, capacity, moe_grad.shape[1])


def body(
    scan_input,
    step_size,
    decay_rate,
    input_proj,
    output_proj,
    skip_gain,
    block_states,
    end_grad,
    scan_grad,
    moe_grad,
    route,
    gate_prob,
    w_down,
    hidden_saved,
):
    inputs = scan_input.astype(jnp.float32)
    steps = step_size.astype(jnp.float32)
    grads = scan_grad.astype(jnp.float32)
    bmats = input_proj.T
    cmats = output_proj.T
    first_state = block_states[0]
    decays = jnp.exp(-steps[:, None, :] * decay_rate[None])
    driving = (steps * inputs)[:, None, :] * bmats[:, :, None]
    sources = cmats[:, :, None] * grads[:, None, :]
    states, seed = local_scans(decays, driving, sources, first_state)
    before = jnp.concatenate([first_state[None], states[:-1]], axis=0)
    out_cols = jnp.sum(states * grads[:, None, :], axis=2)
    shrink = jnp.exp(-decay_rate * jnp.sum(steps, axis=0)[None])
    position = axis_position(CTX)
    count = axis_count(CTX)
    is_last = position == count - 1
    pair = jnp.stack(
        [jnp.where(is_last, 0.0, shrink), jnp.where(is_last, shrink * end_grad + seed, seed)]
    )
    distance = 1
    while distance < count:
        later = shifted_from(pair, CTX, distance)
        present = position + distance < count
        composed = jnp.stack([pair[0] * later[0], pair[0] * later[1] + pair[1]])
        pair = jnp.where(present, composed, pair)
        distance *= 2
    entering = jnp.where(is_last, end_grad, shifted_from(pair[1], CTX, 1))
    adjoint = adjoint_scan(decays, sources, entering)
    input_grad = (
        steps * jnp.sum(bmats[:, :, None] * adjoint, axis=1) + skip_gain[None] * grads
    ).astype(jnp.bfloat16)
    step_grad = jnp.sum(
        adjoint * (bmats[:, :, None] * inputs[:, None, :] - decay_rate[None] * decays * before),
        axis=1,
    ).astype(jnp.bfloat16)
    in_cols = jnp.sum(adjoint * (steps * inputs)[:, None, :], axis=2)
    rate_local = jnp.sum(adjoint * (-steps[:, None, :] * decays * before), axis=0)
    col_sums = jnp.sum(exchange(jnp.stack([in_cols.T, out_cols.T]), ("exp",), True, 1), axis=0)
    in_proj_grad, out_proj_grad = col_sums[0], col_sums[1]
    ctx_count = axis_count(CTX)
    rate_parts = rate_local.reshape(ctx_count, 1, rate_local.size // ctx_count)
    rate_chunk = jnp.sum(exchange(rate_parts, CTX, False, 2), axis=0)
    decay_grad = exchange(rate_chunk, CTX, True, 3).reshape(rate_local.shape)
    slot_total = hidden_saved.shape[1]
    capacity = slot_total // (axis_count(CTX) * lax.axis_size("exp"))
    buffer = slot_buffer(moe_grad, route, gate_prob, capacity)
    received_rows = lax.all_to_all(buffer, "exp", split_axis=0, concat_axis=1, tiled=True)
    plane_rows = lax.all_gather(received_rows, "z", axis=1, tiled=True)
    all_rows = lax.all_gather(plane_rows, "core", axis=1, tiled=True)
    planes, cores = lax.axis_size("z"), lax.axis_size("core")
    grouped = (1, planes, cores, received_rows.shape[1], hidden_saved.shape[2])
    saved_by_core = (
        hidden_saved.reshape(grouped).transpose(0, 2, 1, 3, 4).reshape(hidden_saved.shape)
    )
    weight_total = jnp.einsum(
        "lrf,lrd->lfd", saved_by_core, all_rows, preferred_element_type=jnp.float32
    )
    hidden_by_core = jnp.einsum(
        "lrd,lfd->lrf", all_rows, w_down, preferred_element_type=jnp.float32
    ).astype(jnp.bfloat16)
    hidden_grad = (
        hidden_by_core.reshape(1, cores, planes, received_rows.shape[1], hidden_saved.shape[2])
        .transpose(0, 2, 1, 3, 4)
        .reshape(hidden_saved.shape)
    )
    down_grad = weight_total.astype(jnp.bfloat16)
    return (input_grad, step_grad, in_proj_grad, out_proj_grad, decay_grad, down_grad, hidden_grad)


def solution(mesh):
    placed = (
        P(CTX, "exp"),
        P(CTX, "exp"),
        P(None, "exp"),
        P(None, CTX),
        P(None, CTX),
        P("exp"),
        P(CTX, None, "exp"),
        P(None, "exp"),
        P(CTX, "exp"),
        P(CTX + ("exp",), None),
        P(CTX + ("exp",), None),
        P(CTX + ("exp",), None),
        P("exp", CTX, None),
        P("exp", None, CTX),
    )
    planes = mesh.shape["ctx"] // 2
    split = jax.sharding.Mesh(
        mesh.devices.reshape(planes, 2, mesh.shape["exp"]), CTX + ("exp",)
    )
    return jax.shard_map(
        body,
        mesh=split,
        in_specs=placed,
        out_specs=(
            P(CTX, "exp"),
            P(CTX, "exp"),
            P(None, CTX),
            P(None, CTX),
            P(None, "exp"),
            P("exp", CTX, None),
            P("exp", None, CTX),
        ),
        check_vma=False,
    )
```

```python
import functools

import jax
import jax.numpy as jnp
from jax import lax
from jax.experimental import pallas as pl
from jax.experimental.pallas import tpu as pltpu
from jax.sharding import PartitionSpec as P

EXPERTS = 16


def local_scans_kernel(decay_ref, drive_ref, source_ref, first_ref, states_ref, seed_ref):
    count = decay_ref.shape[0]

    def forward(t, state):
        state = decay_ref[t] * state + drive_ref[t]
        states_ref[t] = state
        return state

    lax.fori_loop(0, count, forward, first_ref[...], unroll=8)

    def backward(i, running):
        t = count - 1 - i
        return decay_ref[t] * (source_ref[t] + running)

    seed_ref[...] = lax.fori_loop(0, count, backward, jnp.zeros_like(first_ref[...]), unroll=8)


def local_scans(decays, driving, sources, first_state):
    return pl.pallas_call(
        local_scans_kernel,
        out_shape=(
            jax.ShapeDtypeStruct(decays.shape, jnp.float32),
            jax.ShapeDtypeStruct(first_state.shape, jnp.float32),
        ),
        cost_estimate=pl.CostEstimate(
            flops=4 * decays.size, bytes_accessed=16 * decays.size, transcendentals=0
        ),
    )(decays, driving, sources, first_state)


def adjoint_scan_kernel(decay_ref, source_ref, entering_ref, adjoint_ref):
    count = decay_ref.shape[0]

    def backward(i, running):
        t = count - 1 - i
        value = source_ref[t] + running
        adjoint_ref[t] = value
        return decay_ref[t] * value

    lax.fori_loop(0, count, backward, entering_ref[...], unroll=8)


def adjoint_scan(decays, sources, entering):
    return pl.pallas_call(
        adjoint_scan_kernel,
        out_shape=jax.ShapeDtypeStruct(decays.shape, jnp.float32),
        cost_estimate=pl.CostEstimate(
            flops=2 * decays.size, bytes_accessed=12 * decays.size, transcendentals=0
        ),
    )(decays, sources, entering)


def exchange_kernel(axis, count, same, x_ref, out_ref, land, send_sems, recv_sems):
    me = lax.axis_index(axis)
    barrier = pltpu.get_barrier_semaphore()
    for k in range(1, count):
        pl.semaphore_signal(
            barrier,
            1,
            device_id={axis: lax.rem(me + k, count)},
            device_id_type=pl.DeviceIdType.MESH,
        )
    pl.semaphore_wait(barrier, count - 1)
    copies = []
    for k in range(1, count):
        peer = lax.rem(me + k, count)
        copy = pltpu.make_async_remote_copy(
            src_ref=x_ref if same else x_ref.at[peer],
            dst_ref=land.at[me],
            send_sem=send_sems.at[k],
            recv_sem=recv_sems.at[k],
            device_id={axis: peer},
            device_id_type=pl.DeviceIdType.MESH,
        )
        copy.start()
        copies.append(copy)
    land[me] = x_ref[...] if same else x_ref[me]
    for copy in copies:
        copy.wait()
    out_ref[...] = land[...]


def exchange(x, axis, same, collective_id):
    count = lax.axis_size(axis)
    block = x.shape if same else x.shape[1:]
    return pl.pallas_call(
        functools.partial(exchange_kernel, axis, count, same),
        out_shape=jax.ShapeDtypeStruct((count,) + block, x.dtype),
        scratch_shapes=[
            pltpu.VMEM((count,) + block, x.dtype),
            pltpu.SemaphoreType.DMA((count,)),
            pltpu.SemaphoreType.DMA((count,)),
        ],
        compiler_params=pltpu.CompilerParams(collective_id=collective_id, has_side_effects=True),
    )(x)


def relay_kernel(axis, count, pair_ref, out_ref, held, land, send_sems, recv_sems):
    me = lax.axis_index(axis)
    distances = []
    while 1 << len(distances) < count:
        distances.append(1 << len(distances))
    land[...] = jnp.zeros_like(land)
    barrier = pltpu.get_barrier_semaphore()
    expected = 0
    for d in distances:

        @pl.when(me >= d)
        def _():
            pl.semaphore_signal(barrier, 1, device_id={axis: me - d}, device_id_type=pl.DeviceIdType.MESH)

        @pl.when(me + d < count)
        def _():
            pl.semaphore_signal(barrier, 1, device_id={axis: me + d}, device_id_type=pl.DeviceIdType.MESH)

        expected = expected + (me >= d).astype(jnp.int32) + (me + d < count).astype(jnp.int32)
    pl.semaphore_wait(barrier, expected)
    rounds = distances + [1]
    for r, d in enumerate(rounds):
        last_round = r == len(rounds) - 1
        source = pair_ref if r == 0 else held.at[r - 1]
        copy = pltpu.make_async_remote_copy(
            src_ref=source,
            dst_ref=land.at[r],
            send_sem=send_sems.at[r],
            recv_sem=recv_sems.at[r],
            device_id={axis: lax.rem(me - d + count, count)},
            device_id_type=pl.DeviceIdType.MESH,
        )

        @pl.when(me >= d)
        def _():
            copy.start()

        if not last_round:
            held[r] = source[...]

        @pl.when(me + d < count)
        def _():
            copy.wait_recv()
            if not last_round:
                shrink, seed = source[0], source[1]
                held[r, 0] = shrink * land[r, 0]
                held[r, 1] = shrink * land[r, 1] + seed

        @pl.when(me >= d)
        def _():
            copy.wait_send()

    out_ref[...] = land[len(rounds) - 1, 1]


def relay(pair, axis, collective_id):
    count = lax.axis_size(axis)
    rounds = max(1, (count - 1).bit_length()) + 1
    return pl.pallas_call(
        functools.partial(relay_kernel, axis, count),
        out_shape=jax.ShapeDtypeStruct(pair.shape[1:], pair.dtype),
        scratch_shapes=[
            pltpu.VMEM((rounds - 1,) + pair.shape, pair.dtype),
            pltpu.VMEM((rounds,) + pair.shape, pair.dtype),
            pltpu.SemaphoreType.DMA((rounds,)),
            pltpu.SemaphoreType.DMA((rounds,)),
        ],
        compiler_params=pltpu.CompilerParams(collective_id=collective_id, has_side_effects=True),
    )(pair)


def slot_buffer(moe_grad, route, gate_prob, capacity):
    pair_count = route.shape[0] * route.shape[1]
    weighted = (gate_prob[:, :, None] * moe_grad.astype(jnp.float32)[:, None, :]).astype(
        jnp.bfloat16
    )
    weighted = weighted.reshape(pair_count, moe_grad.shape[1])
    flat_route = route.reshape(pair_count)
    onehot = (flat_route[:, None] == jnp.arange(EXPERTS, dtype=jnp.int32)[None, :]).astype(
        jnp.int32
    )
    ranks = jnp.sum((jnp.cumsum(onehot, axis=0) - onehot) * onehot, axis=1)
    target = flat_route * capacity + ranks
    placing = (target[:, None] == jnp.arange(EXPERTS * capacity, dtype=jnp.int32)[None, :]).astype(
        jnp.bfloat16
    )
    buffer = jnp.einsum("ps,pd->sd", placing, weighted, preferred_element_type=jnp.float32).astype(
        jnp.bfloat16
    )
    return buffer.reshape(EXPERTS, capacity, moe_grad.shape[1])


def body(
    scan_input,
    step_size,
    decay_rate,
    input_proj,
    output_proj,
    skip_gain,
    block_states,
    end_grad,
    scan_grad,
    moe_grad,
    route,
    gate_prob,
    w_down,
    hidden_saved,
):
    inputs = scan_input.astype(jnp.float32)
    steps = step_size.astype(jnp.float32)
    grads = scan_grad.astype(jnp.float32)
    bmats = input_proj.T
    cmats = output_proj.T
    first_state = block_states[0]
    decays = jnp.exp(-steps[:, None, :] * decay_rate[None])
    driving = (steps * inputs)[:, None, :] * bmats[:, :, None]
    sources = cmats[:, :, None] * grads[:, None, :]
    states, seed = local_scans(decays, driving, sources, first_state)
    before = jnp.concatenate([first_state[None], states[:-1]], axis=0)
    out_cols = jnp.sum(states * grads[:, None, :], axis=2)
    shrink = jnp.exp(-decay_rate * jnp.sum(steps, axis=0)[None])
    position = lax.axis_index("ctx")
    count = lax.axis_size("ctx")
    is_last = position == count - 1
    pair = jnp.stack(
        [jnp.where(is_last, 0.0, shrink), jnp.where(is_last, shrink * end_grad + seed, seed)]
    )
    entering = jnp.where(is_last, end_grad, relay(pair, "ctx", 4))
    adjoint = adjoint_scan(decays, sources, entering)
    input_grad = (
        steps * jnp.sum(bmats[:, :, None] * adjoint, axis=1) + skip_gain[None] * grads
    ).astype(jnp.bfloat16)
    step_grad = jnp.sum(
        adjoint * (bmats[:, :, None] * inputs[:, None, :] - decay_rate[None] * decays * before),
        axis=1,
    ).astype(jnp.bfloat16)
    in_cols = jnp.sum(adjoint * (steps * inputs)[:, None, :], axis=2)
    rate_local = jnp.sum(adjoint * (-steps[:, None, :] * decays * before), axis=0)
    col_sums = jnp.sum(exchange(jnp.stack([in_cols.T, out_cols.T]), "exp", True, 1), axis=0)
    in_proj_grad, out_proj_grad = col_sums[0], col_sums[1]
    ctx_count = lax.axis_size("ctx")
    rate_parts = rate_local.reshape(ctx_count, 1, rate_local.size // ctx_count)
    rate_chunk = jnp.sum(exchange(rate_parts, "ctx", False, 2), axis=0)
    decay_grad = exchange(rate_chunk, "ctx", True, 3).reshape(rate_local.shape)
    slot_total = hidden_saved.shape[1]
    capacity = slot_total // (lax.axis_size("ctx") * lax.axis_size("exp"))
    buffer = slot_buffer(moe_grad, route, gate_prob, capacity)
    received_rows = lax.all_to_all(buffer, "exp", split_axis=0, concat_axis=1, tiled=True)
    all_rows = lax.all_gather(received_rows, "ctx", axis=1, tiled=True)
    weight_total = jnp.einsum(
        "lrf,lrd->lfd", hidden_saved, all_rows, preferred_element_type=jnp.float32
    )
    hidden_grad = jnp.einsum(
        "lrd,lfd->lrf", all_rows, w_down, preferred_element_type=jnp.float32
    ).astype(jnp.bfloat16)
    down_grad = weight_total.astype(jnp.bfloat16)
    return (input_grad, step_grad, in_proj_grad, out_proj_grad, decay_grad, down_grad, hidden_grad)


def solution(mesh):
    placed = (
        P("ctx", "exp"),
        P("ctx", "exp"),
        P(None, "exp"),
        P(None, "ctx"),
        P(None, "ctx"),
        P("exp"),
        P("ctx", None, "exp"),
        P(None, "exp"),
        P("ctx", "exp"),
        P(("ctx", "exp"), None),
        P(("ctx", "exp"), None),
        P(("ctx", "exp"), None),
        P("exp", "ctx", None),
        P("exp", None, "ctx"),
    )
    return jax.shard_map(
        body,
        mesh=mesh,
        in_specs=placed,
        out_specs=(
            P("ctx", "exp"),
            P("ctx", "exp"),
            P(None, "ctx"),
            P(None, "ctx"),
            P(None, "exp"),
            P("exp", "ctx", None),
            P("exp", None, "ctx"),
        ),
        check_vma=False,
    )
```

```python
import functools

import jax
import jax.numpy as jnp
from jax import lax
from jax.experimental import pallas as pl
from jax.experimental.pallas import tpu as pltpu
from jax.sharding import PartitionSpec as P

EXPERTS = 16


def local_scans_kernel(decay_ref, drive_ref, source_ref, first_ref, states_ref, seed_ref):
    count = decay_ref.shape[0]

    def forward(t, state):
        state = decay_ref[t] * state + drive_ref[t]
        states_ref[t] = state
        return state

    lax.fori_loop(0, count, forward, first_ref[...], unroll=8)

    def backward(i, running):
        t = count - 1 - i
        return decay_ref[t] * (source_ref[t] + running)

    seed_ref[...] = lax.fori_loop(0, count, backward, jnp.zeros_like(first_ref[...]), unroll=8)


def local_scans(decays, driving, sources, first_state):
    return pl.pallas_call(
        local_scans_kernel,
        out_shape=(
            jax.ShapeDtypeStruct(decays.shape, jnp.float32),
            jax.ShapeDtypeStruct(first_state.shape, jnp.float32),
        ),
        cost_estimate=pl.CostEstimate(
            flops=4 * decays.size, bytes_accessed=16 * decays.size, transcendentals=0
        ),
    )(decays, driving, sources, first_state)


def adjoint_scan_kernel(decay_ref, source_ref, entering_ref, adjoint_ref):
    count = decay_ref.shape[0]

    def backward(i, running):
        t = count - 1 - i
        value = source_ref[t] + running
        adjoint_ref[t] = value
        return decay_ref[t] * value

    lax.fori_loop(0, count, backward, entering_ref[...], unroll=8)


def adjoint_scan(decays, sources, entering):
    return pl.pallas_call(
        adjoint_scan_kernel,
        out_shape=jax.ShapeDtypeStruct(decays.shape, jnp.float32),
        cost_estimate=pl.CostEstimate(
            flops=2 * decays.size, bytes_accessed=12 * decays.size, transcendentals=0
        ),
    )(decays, sources, entering)


def relay_kernel(axis, count, pair_ref, out_ref, held, land, send_sems, recv_sems):
    me = lax.axis_index(axis)
    distances = []
    while 1 << len(distances) < count:
        distances.append(1 << len(distances))
    land[...] = jnp.zeros_like(land)
    barrier = pltpu.get_barrier_semaphore()
    expected = 0
    for d in distances:

        @pl.when(me >= d)
        def _():
            pl.semaphore_signal(barrier, 1, device_id={axis: me - d}, device_id_type=pl.DeviceIdType.MESH)

        @pl.when(me + d < count)
        def _():
            pl.semaphore_signal(barrier, 1, device_id={axis: me + d}, device_id_type=pl.DeviceIdType.MESH)

        expected = expected + (me >= d).astype(jnp.int32) + (me + d < count).astype(jnp.int32)
    pl.semaphore_wait(barrier, expected)
    rounds = distances + [1]
    for r, d in enumerate(rounds):
        last_round = r == len(rounds) - 1
        source = pair_ref if r == 0 else held.at[r - 1]
        copy = pltpu.make_async_remote_copy(
            src_ref=source,
            dst_ref=land.at[r],
            send_sem=send_sems.at[r],
            recv_sem=recv_sems.at[r],
            device_id={axis: lax.rem(me - d + count, count)},
            device_id_type=pl.DeviceIdType.MESH,
        )

        @pl.when(me >= d)
        def _():
            copy.start()

        if not last_round:
            held[r] = source[...]

        @pl.when(me + d < count)
        def _():
            copy.wait_recv()
            if not last_round:
                shrink, seed = source[0], source[1]
                held[r, 0] = shrink * land[r, 0]
                held[r, 1] = shrink * land[r, 1] + seed

        @pl.when(me >= d)
        def _():
            copy.wait_send()

    out_ref[...] = land[len(rounds) - 1, 1]


def relay(pair, axis, collective_id):
    count = lax.axis_size(axis)
    rounds = max(1, (count - 1).bit_length()) + 1
    return pl.pallas_call(
        functools.partial(relay_kernel, axis, count),
        out_shape=jax.ShapeDtypeStruct(pair.shape[1:], pair.dtype),
        scratch_shapes=[
            pltpu.VMEM((rounds - 1,) + pair.shape, pair.dtype),
            pltpu.VMEM((rounds,) + pair.shape, pair.dtype),
            pltpu.SemaphoreType.DMA((rounds,)),
            pltpu.SemaphoreType.DMA((rounds,)),
        ],
        compiler_params=pltpu.CompilerParams(collective_id=collective_id, has_side_effects=True),
    )(pair)


def reduce_kernel(cols_ref, parts_ref, cols_out, rate_out, cols_land, parts_land, chunk, chunk_land, sems):
    me_e, me_c = lax.axis_index("exp"), lax.axis_index("ctx")
    n_e, n_c = lax.axis_size("exp"), lax.axis_size("ctx")
    mesh_id = pl.DeviceIdType.MESH
    barrier = pltpu.get_barrier_semaphore()
    for k in range(1, n_e):
        pl.semaphore_signal(barrier, 1, device_id={"exp": lax.rem(me_e + k, n_e)}, device_id_type=mesh_id)
    for k in range(1, n_c):
        pl.semaphore_signal(barrier, 1, device_id={"ctx": lax.rem(me_c + k, n_c)}, device_id_type=mesh_id)
    pl.semaphore_wait(barrier, n_e - 1 + n_c - 1)

    def push(src, dst, axis, peer, slot):
        copy = pltpu.make_async_remote_copy(
            src_ref=src,
            dst_ref=dst,
            send_sem=sems.at[0, slot],
            recv_sem=sems.at[1, slot],
            device_id={axis: peer},
            device_id_type=mesh_id,
        )
        copy.start()
        return copy

    scattered = [
        push(parts_ref.at[lax.rem(me_c + k, n_c)], parts_land.at[me_c], "ctx", lax.rem(me_c + k, n_c), k)
        for k in range(1, n_c)
    ]
    gathered = [
        push(cols_ref, cols_land.at[me_e], "exp", lax.rem(me_e + k, n_e), 2 * n_c + k)
        for k in range(1, n_e)
    ]
    parts_land[me_c] = parts_ref[me_c]
    cols_land[me_e] = cols_ref[...]
    for copy in scattered:
        copy.wait()
    chunk[...] = jnp.sum(parts_land[...], axis=0)
    chunk_land[me_c] = chunk[...]
    spread = [
        push(chunk, chunk_land.at[me_c], "ctx", lax.rem(me_c + k, n_c), n_c + k)
        for k in range(1, n_c)
    ]
    for copy in gathered + spread:
        copy.wait()
    cols_out[...] = cols_land[...]
    rate_out[...] = chunk_land[...]


def reduce_partials(cols, parts, collective_id):
    n_e, n_c = lax.axis_size("exp"), lax.axis_size("ctx")
    return pl.pallas_call(
        reduce_kernel,
        out_shape=(
            jax.ShapeDtypeStruct((n_e,) + cols.shape, cols.dtype),
            jax.ShapeDtypeStruct(parts.shape, parts.dtype),
        ),
        scratch_shapes=[
            pltpu.VMEM((n_e,) + cols.shape, cols.dtype),
            pltpu.VMEM(parts.shape, parts.dtype),
            pltpu.VMEM(parts.shape[1:], parts.dtype),
            pltpu.VMEM(parts.shape, parts.dtype),
            pltpu.SemaphoreType.DMA((2, 2 * n_c + n_e)),
        ],
        compiler_params=pltpu.CompilerParams(collective_id=collective_id, has_side_effects=True),
    )(cols, parts)


def slot_buffer(moe_grad, route, gate_prob, capacity):
    pair_count = route.shape[0] * route.shape[1]
    weighted = (gate_prob[:, :, None] * moe_grad.astype(jnp.float32)[:, None, :]).astype(
        jnp.bfloat16
    )
    weighted = weighted.reshape(pair_count, moe_grad.shape[1])
    flat_route = route.reshape(pair_count)
    onehot = (flat_route[:, None] == jnp.arange(EXPERTS, dtype=jnp.int32)[None, :]).astype(
        jnp.int32
    )
    ranks = jnp.sum((jnp.cumsum(onehot, axis=0) - onehot) * onehot, axis=1)
    target = flat_route * capacity + ranks
    placing = (target[:, None] == jnp.arange(EXPERTS * capacity, dtype=jnp.int32)[None, :]).astype(
        jnp.bfloat16
    )
    buffer = jnp.einsum("ps,pd->sd", placing, weighted, preferred_element_type=jnp.float32).astype(
        jnp.bfloat16
    )
    return buffer.reshape(EXPERTS, capacity, moe_grad.shape[1])


def body(
    scan_input,
    step_size,
    decay_rate,
    input_proj,
    output_proj,
    skip_gain,
    block_states,
    end_grad,
    scan_grad,
    moe_grad,
    route,
    gate_prob,
    w_down,
    hidden_saved,
):
    inputs = scan_input.astype(jnp.float32)
    steps = step_size.astype(jnp.float32)
    grads = scan_grad.astype(jnp.float32)
    bmats = input_proj.T
    cmats = output_proj.T
    first_state = block_states[0]
    decays = jnp.exp(-steps[:, None, :] * decay_rate[None])
    driving = (steps * inputs)[:, None, :] * bmats[:, :, None]
    sources = cmats[:, :, None] * grads[:, None, :]
    states, seed = local_scans(decays, driving, sources, first_state)
    before = jnp.concatenate([first_state[None], states[:-1]], axis=0)
    out_cols = jnp.sum(states * grads[:, None, :], axis=2)
    shrink = jnp.exp(-decay_rate * jnp.sum(steps, axis=0)[None])
    position = lax.axis_index("ctx")
    count = lax.axis_size("ctx")
    is_last = position == count - 1
    pair = jnp.stack(
        [jnp.where(is_last, 0.0, shrink), jnp.where(is_last, shrink * end_grad + seed, seed)]
    )
    entering = jnp.where(is_last, end_grad, relay(pair, "ctx", 4))
    adjoint = adjoint_scan(decays, sources, entering)
    input_grad = (
        steps * jnp.sum(bmats[:, :, None] * adjoint, axis=1) + skip_gain[None] * grads
    ).astype(jnp.bfloat16)
    step_grad = jnp.sum(
        adjoint * (bmats[:, :, None] * inputs[:, None, :] - decay_rate[None] * decays * before),
        axis=1,
    ).astype(jnp.bfloat16)
    in_cols = jnp.sum(adjoint * (steps * inputs)[:, None, :], axis=2)
    rate_local = jnp.sum(adjoint * (-steps[:, None, :] * decays * before), axis=0)
    ctx_count = lax.axis_size("ctx")
    rate_parts = rate_local.reshape(ctx_count, 1, rate_local.size // ctx_count)
    col_parts, rate_chunks = reduce_partials(jnp.stack([in_cols.T, out_cols.T]), rate_parts, 1)
    col_sums = jnp.sum(col_parts, axis=0)
    in_proj_grad, out_proj_grad = col_sums[0], col_sums[1]
    decay_grad = rate_chunks.reshape(rate_local.shape)
    slot_total = hidden_saved.shape[1]
    capacity = slot_total // (lax.axis_size("ctx") * lax.axis_size("exp"))
    buffer = slot_buffer(moe_grad, route, gate_prob, capacity)
    received_rows = lax.all_to_all(buffer, "exp", split_axis=0, concat_axis=1, tiled=True)
    all_rows = lax.all_gather(received_rows, "ctx", axis=1, tiled=True)
    weight_total = jnp.einsum(
        "lrf,lrd->lfd", hidden_saved, all_rows, preferred_element_type=jnp.float32
    )
    hidden_grad = jnp.einsum(
        "lrd,lfd->lrf", all_rows, w_down, preferred_element_type=jnp.float32
    ).astype(jnp.bfloat16)
    down_grad = weight_total.astype(jnp.bfloat16)
    return (input_grad, step_grad, in_proj_grad, out_proj_grad, decay_grad, down_grad, hidden_grad)


def solution(mesh):
    placed = (
        P("ctx", "exp"),
        P("ctx", "exp"),
        P(None, "exp"),
        P(None, "ctx"),
        P(None, "ctx"),
        P("exp"),
        P("ctx", None, "exp"),
        P(None, "exp"),
        P("ctx", "exp"),
        P(("ctx", "exp"), None),
        P(("ctx", "exp"), None),
        P(("ctx", "exp"), None),
        P("exp", "ctx", None),
        P("exp", None, "ctx"),
    )
    return jax.shard_map(
        body,
        mesh=mesh,
        in_specs=placed,
        out_specs=(
            P("ctx", "exp"),
            P("ctx", "exp"),
            P(None, "ctx"),
            P(None, "ctx"),
            P(None, "exp"),
            P("exp", "ctx", None),
            P("exp", None, "ctx"),
        ),
        check_vma=False,
    )
```

```python
import functools

import jax
import jax.numpy as jnp
from jax import lax
from jax.experimental import pallas as pl
from jax.experimental.pallas import tpu as pltpu
from jax.sharding import PartitionSpec as P

EXPERTS = 16


def local_scans_kernel(decay_ref, drive_ref, source_ref, first_ref, states_ref, seed_ref):
    count = decay_ref.shape[0]

    def forward(t, state):
        state = decay_ref[t] * state + drive_ref[t]
        states_ref[t] = state
        return state

    lax.fori_loop(0, count, forward, first_ref[...], unroll=8)

    def backward(i, running):
        t = count - 1 - i
        return decay_ref[t] * (source_ref[t] + running)

    seed_ref[...] = lax.fori_loop(0, count, backward, jnp.zeros_like(first_ref[...]), unroll=8)


def local_scans(decays, driving, sources, first_state):
    return pl.pallas_call(
        local_scans_kernel,
        out_shape=(
            jax.ShapeDtypeStruct(decays.shape, jnp.float32),
            jax.ShapeDtypeStruct(first_state.shape, jnp.float32),
        ),
        cost_estimate=pl.CostEstimate(
            flops=4 * decays.size, bytes_accessed=16 * decays.size, transcendentals=0
        ),
    )(decays, driving, sources, first_state)


def adjoint_scan_kernel(decay_ref, source_ref, entering_ref, adjoint_ref):
    count = decay_ref.shape[0]

    def backward(i, running):
        t = count - 1 - i
        value = source_ref[t] + running
        adjoint_ref[t] = value
        return decay_ref[t] * value

    lax.fori_loop(0, count, backward, entering_ref[...], unroll=8)


def adjoint_scan(decays, sources, entering):
    return pl.pallas_call(
        adjoint_scan_kernel,
        out_shape=jax.ShapeDtypeStruct(decays.shape, jnp.float32),
        cost_estimate=pl.CostEstimate(
            flops=2 * decays.size, bytes_accessed=12 * decays.size, transcendentals=0
        ),
    )(decays, sources, entering)


def relay_kernel(axis, count, radix, pair_ref, out_ref, held, land, send_sems, recv_sems):
    me = lax.axis_index(axis)
    mesh_id = pl.DeviceIdType.MESH
    distances = [1]
    while distances[-1] * radix < count:
        distances.append(distances[-1] * radix)
    offsets = sorted({d * m for d in distances for m in range(1, radix)})
    land[...] = jnp.zeros_like(land)
    barrier = pltpu.get_barrier_semaphore()
    expected = 0
    for o in offsets:

        @pl.when(me >= o)
        def _():
            pl.semaphore_signal(barrier, 1, device_id={axis: me - o}, device_id_type=mesh_id)

        @pl.when(me + o < count)
        def _():
            pl.semaphore_signal(barrier, 1, device_id={axis: me + o}, device_id_type=mesh_id)

        expected = expected + (me >= o).astype(jnp.int32) + (me + o < count).astype(jnp.int32)
    pl.semaphore_wait(barrier, expected)
    slot = 0
    for r, d in enumerate(distances):
        source = pair_ref if r == 0 else held.at[r - 1]
        copies = []
        for m in range(1, radix):
            o = d * m
            copy = pltpu.make_async_remote_copy(
                src_ref=source,
                dst_ref=land.at[slot],
                send_sem=send_sems.at[slot],
                recv_sem=recv_sems.at[slot],
                device_id={axis: lax.rem(me - o + count, count)},
                device_id_type=mesh_id,
            )
            copies.append((o, slot, copy))
            slot += 1

            @pl.when(me >= o)
            def _():
                copy.start()

        held[r] = source[...]
        for o, s, copy in copies:

            @pl.when(me + o < count)
            def _():
                copy.wait_recv()
                shrink, seed = held[r, 0], held[r, 1]
                held[r, 0] = shrink * land[s, 0]
                held[r, 1] = shrink * land[s, 1] + seed

        for o, s, copy in copies:

            @pl.when(me >= o)
            def _():
                copy.wait_send()

    last = len(distances) - 1
    shift = pltpu.make_async_remote_copy(
        src_ref=held.at[last],
        dst_ref=land.at[slot],
        send_sem=send_sems.at[slot],
        recv_sem=recv_sems.at[slot],
        device_id={axis: lax.rem(me - 1 + count, count)},
        device_id_type=mesh_id,
    )

    @pl.when(me >= 1)
    def _():
        shift.start()

    @pl.when(me + 1 < count)
    def _():
        shift.wait_recv()

    @pl.when(me >= 1)
    def _():
        shift.wait_send()

    out_ref[...] = land[slot, 1]


def relay(pair, axis, collective_id, radix=4):
    count = lax.axis_size(axis)
    rounds = 1
    while radix**rounds < count:
        rounds += 1
    slots = rounds * (radix - 1) + 1
    return pl.pallas_call(
        functools.partial(relay_kernel, axis, count, radix),
        out_shape=jax.ShapeDtypeStruct(pair.shape[1:], pair.dtype),
        scratch_shapes=[
            pltpu.VMEM((rounds,) + pair.shape, pair.dtype),
            pltpu.VMEM((slots,) + pair.shape, pair.dtype),
            pltpu.SemaphoreType.DMA((slots,)),
            pltpu.SemaphoreType.DMA((slots,)),
        ],
        compiler_params=pltpu.CompilerParams(collective_id=collective_id, has_side_effects=True),
    )(pair)


def reduce_kernel(cols_ref, parts_ref, cols_out, rate_out, cols_land, parts_land, chunk, chunk_land, sems):
    me_e, me_c = lax.axis_index("exp"), lax.axis_index("ctx")
    n_e, n_c = lax.axis_size("exp"), lax.axis_size("ctx")
    mesh_id = pl.DeviceIdType.MESH
    barrier = pltpu.get_barrier_semaphore()
    for k in range(1, n_e):
        pl.semaphore_signal(barrier, 1, device_id={"exp": lax.rem(me_e + k, n_e)}, device_id_type=mesh_id)
    for k in range(1, n_c):
        pl.semaphore_signal(barrier, 1, device_id={"ctx": lax.rem(me_c + k, n_c)}, device_id_type=mesh_id)
    pl.semaphore_wait(barrier, n_e - 1 + n_c - 1)

    def push(src, dst, axis, peer, slot):
        copy = pltpu.make_async_remote_copy(
            src_ref=src,
            dst_ref=dst,
            send_sem=sems.at[0, slot],
            recv_sem=sems.at[1, slot],
            device_id={axis: peer},
            device_id_type=mesh_id,
        )
        copy.start()
        return copy

    scattered = [
        push(parts_ref.at[lax.rem(me_c + k, n_c)], parts_land.at[me_c], "ctx", lax.rem(me_c + k, n_c), k)
        for k in range(1, n_c)
    ]
    gathered = [
        push(cols_ref, cols_land.at[me_e], "exp", lax.rem(me_e + k, n_e), 2 * n_c + k)
        for k in range(1, n_e)
    ]
    parts_land[me_c] = parts_ref[me_c]
    cols_land[me_e] = cols_ref[...]
    for copy in scattered:
        copy.wait()
    chunk[...] = jnp.sum(parts_land[...], axis=0)
    chunk_land[me_c] = chunk[...]
    spread = [
        push(chunk, chunk_land.at[me_c], "ctx", lax.rem(me_c + k, n_c), n_c + k)
        for k in range(1, n_c)
    ]
    for copy in gathered + spread:
        copy.wait()
    cols_out[...] = cols_land[...]
    rate_out[...] = chunk_land[...]


def reduce_partials(cols, parts, collective_id):
    n_e, n_c = lax.axis_size("exp"), lax.axis_size("ctx")
    return pl.pallas_call(
        reduce_kernel,
        out_shape=(
            jax.ShapeDtypeStruct((n_e,) + cols.shape, cols.dtype),
            jax.ShapeDtypeStruct(parts.shape, parts.dtype),
        ),
        scratch_shapes=[
            pltpu.VMEM((n_e,) + cols.shape, cols.dtype),
            pltpu.VMEM(parts.shape, parts.dtype),
            pltpu.VMEM(parts.shape[1:], parts.dtype),
            pltpu.VMEM(parts.shape, parts.dtype),
            pltpu.SemaphoreType.DMA((2, 2 * n_c + n_e)),
        ],
        compiler_params=pltpu.CompilerParams(collective_id=collective_id, has_side_effects=True),
    )(cols, parts)


def slot_buffer(moe_grad, route, gate_prob, capacity):
    pair_count = route.shape[0] * route.shape[1]
    weighted = (gate_prob[:, :, None] * moe_grad.astype(jnp.float32)[:, None, :]).astype(
        jnp.bfloat16
    )
    weighted = weighted.reshape(pair_count, moe_grad.shape[1])
    flat_route = route.reshape(pair_count)
    onehot = (flat_route[:, None] == jnp.arange(EXPERTS, dtype=jnp.int32)[None, :]).astype(
        jnp.int32
    )
    ranks = jnp.sum((jnp.cumsum(onehot, axis=0) - onehot) * onehot, axis=1)
    target = flat_route * capacity + ranks
    placing = (target[:, None] == jnp.arange(EXPERTS * capacity, dtype=jnp.int32)[None, :]).astype(
        jnp.bfloat16
    )
    buffer = jnp.einsum("ps,pd->sd", placing, weighted, preferred_element_type=jnp.float32).astype(
        jnp.bfloat16
    )
    return buffer.reshape(EXPERTS, capacity, moe_grad.shape[1])


def body(
    scan_input,
    step_size,
    decay_rate,
    input_proj,
    output_proj,
    skip_gain,
    block_states,
    end_grad,
    scan_grad,
    moe_grad,
    route,
    gate_prob,
    w_down,
    hidden_saved,
):
    inputs = scan_input.astype(jnp.float32)
    steps = step_size.astype(jnp.float32)
    grads = scan_grad.astype(jnp.float32)
    bmats = input_proj.T
    cmats = output_proj.T
    first_state = block_states[0]
    decays = jnp.exp(-steps[:, None, :] * decay_rate[None])
    driving = (steps * inputs)[:, None, :] * bmats[:, :, None]
    sources = cmats[:, :, None] * grads[:, None, :]
    states, seed = local_scans(decays, driving, sources, first_state)
    before = jnp.concatenate([first_state[None], states[:-1]], axis=0)
    out_cols = jnp.sum(states * grads[:, None, :], axis=2)
    shrink = jnp.exp(-decay_rate * jnp.sum(steps, axis=0)[None])
    position = lax.axis_index("ctx")
    count = lax.axis_size("ctx")
    is_last = position == count - 1
    pair = jnp.stack(
        [jnp.where(is_last, 0.0, shrink), jnp.where(is_last, shrink * end_grad + seed, seed)]
    )
    entering = jnp.where(is_last, end_grad, relay(pair, "ctx", 4))
    adjoint = adjoint_scan(decays, sources, entering)
    input_grad = (
        steps * jnp.sum(bmats[:, :, None] * adjoint, axis=1) + skip_gain[None] * grads
    ).astype(jnp.bfloat16)
    step_grad = jnp.sum(
        adjoint * (bmats[:, :, None] * inputs[:, None, :] - decay_rate[None] * decays * before),
        axis=1,
    ).astype(jnp.bfloat16)
    in_cols = jnp.sum(adjoint * (steps * inputs)[:, None, :], axis=2)
    rate_local = jnp.sum(adjoint * (-steps[:, None, :] * decays * before), axis=0)
    ctx_count = lax.axis_size("ctx")
    rate_parts = rate_local.reshape(ctx_count, 1, rate_local.size // ctx_count)
    col_parts, rate_chunks = reduce_partials(jnp.stack([in_cols.T, out_cols.T]), rate_parts, 1)
    col_sums = jnp.sum(col_parts, axis=0)
    in_proj_grad, out_proj_grad = col_sums[0], col_sums[1]
    decay_grad = rate_chunks.reshape(rate_local.shape)
    slot_total = hidden_saved.shape[1]
    capacity = slot_total // (lax.axis_size("ctx") * lax.axis_size("exp"))
    buffer = slot_buffer(moe_grad, route, gate_prob, capacity)
    received_rows = lax.all_to_all(buffer, "exp", split_axis=0, concat_axis=1, tiled=True)
    all_rows = lax.all_gather(received_rows, "ctx", axis=1, tiled=True)
    weight_total = jnp.einsum(
        "lrf,lrd->lfd", hidden_saved, all_rows, preferred_element_type=jnp.float32
    )
    hidden_grad = jnp.einsum(
        "lrd,lfd->lrf", all_rows, w_down, preferred_element_type=jnp.float32
    ).astype(jnp.bfloat16)
    down_grad = weight_total.astype(jnp.bfloat16)
    return (input_grad, step_grad, in_proj_grad, out_proj_grad, decay_grad, down_grad, hidden_grad)


def solution(mesh):
    placed = (
        P("ctx", "exp"),
        P("ctx", "exp"),
        P(None, "exp"),
        P(None, "ctx"),
        P(None, "ctx"),
        P("exp"),
        P("ctx", None, "exp"),
        P(None, "exp"),
        P("ctx", "exp"),
        P(("ctx", "exp"), None),
        P(("ctx", "exp"), None),
        P(("ctx", "exp"), None),
        P("exp", "ctx", None),
        P("exp", None, "ctx"),
    )
    return jax.shard_map(
        body,
        mesh=mesh,
        in_specs=placed,
        out_specs=(
            P("ctx", "exp"),
            P("ctx", "exp"),
            P(None, "ctx"),
            P(None, "ctx"),
            P(None, "exp"),
            P("exp", "ctx", None),
            P("exp", None, "ctx"),
        ),
        check_vma=False,
    )
```

```python
import functools

import jax
import jax.numpy as jnp
from jax import lax
from jax.experimental import pallas as pl
from jax.experimental.pallas import tpu as pltpu
from jax.sharding import PartitionSpec as P

EXPERTS = 16


def local_scans_kernel(decay_ref, drive_ref, source_ref, first_ref, states_ref, seed_ref):
    count = decay_ref.shape[0]

    def forward(t, state):
        state = decay_ref[t] * state + drive_ref[t]
        states_ref[t] = state
        return state

    lax.fori_loop(0, count, forward, first_ref[...], unroll=8)

    def backward(i, running):
        t = count - 1 - i
        return decay_ref[t] * (source_ref[t] + running)

    seed_ref[...] = lax.fori_loop(0, count, backward, jnp.zeros_like(first_ref[...]), unroll=8)


def local_scans(decays, driving, sources, first_state):
    return pl.pallas_call(
        local_scans_kernel,
        out_shape=(
            jax.ShapeDtypeStruct(decays.shape, jnp.float32),
            jax.ShapeDtypeStruct(first_state.shape, jnp.float32),
        ),
        cost_estimate=pl.CostEstimate(
            flops=4 * decays.size, bytes_accessed=16 * decays.size, transcendentals=0
        ),
    )(decays, driving, sources, first_state)


def adjoint_scan_kernel(decay_ref, source_ref, entering_ref, adjoint_ref):
    count = decay_ref.shape[0]

    def backward(i, running):
        t = count - 1 - i
        value = source_ref[t] + running
        adjoint_ref[t] = value
        return decay_ref[t] * value

    lax.fori_loop(0, count, backward, entering_ref[...], unroll=8)


def adjoint_scan(decays, sources, entering):
    return pl.pallas_call(
        adjoint_scan_kernel,
        out_shape=jax.ShapeDtypeStruct(decays.shape, jnp.float32),
        cost_estimate=pl.CostEstimate(
            flops=2 * decays.size, bytes_accessed=12 * decays.size, transcendentals=0
        ),
    )(decays, sources, entering)


def relay_kernel(
    axis, count, radix, pair_ref, rows_ref, out_ref, all_rows, held, land, send_sems, recv_sems, row_sems
):
    me = lax.axis_index(axis)
    mesh_id = pl.DeviceIdType.MESH
    distances = [1]
    while distances[-1] * radix < count:
        distances.append(distances[-1] * radix)
    offsets = sorted({d * m for d in distances for m in range(1, radix)})
    land[...] = jnp.zeros_like(land)
    barrier = pltpu.get_barrier_semaphore()
    for k in range(1, count):
        pl.semaphore_signal(
            barrier, 1, device_id={axis: lax.rem(me + k, count)}, device_id_type=mesh_id
        )
    pl.semaphore_wait(barrier, count - 1)
    block = rows_ref.shape[1]
    row_copies = []
    for k in range(1, count):
        copy = pltpu.make_async_remote_copy(
            src_ref=rows_ref,
            dst_ref=all_rows.at[:, pl.ds(me * block, block)],
            send_sem=row_sems.at[0, k],
            recv_sem=row_sems.at[1, k],
            device_id={axis: lax.rem(me + k, count)},
            device_id_type=mesh_id,
        )
        copy.start()
        row_copies.append(copy)
    own = pltpu.make_async_copy(rows_ref, all_rows.at[:, pl.ds(me * block, block)], row_sems.at[0, 0])
    own.start()
    slot = 0
    for r, d in enumerate(distances):
        source = pair_ref if r == 0 else held.at[r - 1]
        copies = []
        for m in range(1, radix):
            o = d * m
            copy = pltpu.make_async_remote_copy(
                src_ref=source,
                dst_ref=land.at[slot],
                send_sem=send_sems.at[slot],
                recv_sem=recv_sems.at[slot],
                device_id={axis: lax.rem(me - o + count, count)},
                device_id_type=mesh_id,
            )
            copies.append((o, slot, copy))
            slot += 1

            @pl.when(me >= o)
            def _():
                copy.start()

        held[r] = source[...]
        for o, s, copy in copies:

            @pl.when(me + o < count)
            def _():
                copy.wait_recv()
                shrink, seed = held[r, 0], held[r, 1]
                held[r, 0] = shrink * land[s, 0]
                held[r, 1] = shrink * land[s, 1] + seed

        for o, s, copy in copies:

            @pl.when(me >= o)
            def _():
                copy.wait_send()

    last = len(distances) - 1
    shift = pltpu.make_async_remote_copy(
        src_ref=held.at[last],
        dst_ref=land.at[slot],
        send_sem=send_sems.at[slot],
        recv_sem=recv_sems.at[slot],
        device_id={axis: lax.rem(me - 1 + count, count)},
        device_id_type=mesh_id,
    )

    @pl.when(me >= 1)
    def _():
        shift.start()

    @pl.when(me + 1 < count)
    def _():
        shift.wait_recv()

    @pl.when(me >= 1)
    def _():
        shift.wait_send()

    out_ref[...] = land[slot, 1]
    own.wait()
    for copy in row_copies:
        copy.wait()


def relay(pair, rows, axis, collective_id, radix=4):
    count = lax.axis_size(axis)
    rounds = 1
    while radix**rounds < count:
        rounds += 1
    slots = rounds * (radix - 1) + 1
    return pl.pallas_call(
        functools.partial(relay_kernel, axis, count, radix),
        out_shape=(
            jax.ShapeDtypeStruct(pair.shape[1:], pair.dtype),
            jax.ShapeDtypeStruct((rows.shape[0], count * rows.shape[1]) + rows.shape[2:], rows.dtype),
        ),
        in_specs=[pl.BlockSpec(memory_space=pltpu.VMEM), pl.BlockSpec(memory_space=pl.ANY)],
        out_specs=(pl.BlockSpec(memory_space=pltpu.VMEM), pl.BlockSpec(memory_space=pl.ANY)),
        scratch_shapes=[
            pltpu.VMEM((rounds,) + pair.shape, pair.dtype),
            pltpu.VMEM((slots,) + pair.shape, pair.dtype),
            pltpu.SemaphoreType.DMA((slots,)),
            pltpu.SemaphoreType.DMA((slots,)),
            pltpu.SemaphoreType.DMA((2, count)),
        ],
        compiler_params=pltpu.CompilerParams(collective_id=collective_id, has_side_effects=True),
    )(pair, rows)


def reduce_kernel(cols_ref, parts_ref, cols_out, rate_out, cols_land, parts_land, chunk, chunk_land, sems):
    me_e, me_c = lax.axis_index("exp"), lax.axis_index("ctx")
    n_e, n_c = lax.axis_size("exp"), lax.axis_size("ctx")
    mesh_id = pl.DeviceIdType.MESH
    barrier = pltpu.get_barrier_semaphore()
    for k in range(1, n_e):
        pl.semaphore_signal(barrier, 1, device_id={"exp": lax.rem(me_e + k, n_e)}, device_id_type=mesh_id)
    for k in range(1, n_c):
        pl.semaphore_signal(barrier, 1, device_id={"ctx": lax.rem(me_c + k, n_c)}, device_id_type=mesh_id)
    pl.semaphore_wait(barrier, n_e - 1 + n_c - 1)

    def push(src, dst, axis, peer, slot):
        copy = pltpu.make_async_remote_copy(
            src_ref=src,
            dst_ref=dst,
            send_sem=sems.at[0, slot],
            recv_sem=sems.at[1, slot],
            device_id={axis: peer},
            device_id_type=mesh_id,
        )
        copy.start()
        return copy

    scattered = [
        push(parts_ref.at[lax.rem(me_c + k, n_c)], parts_land.at[me_c], "ctx", lax.rem(me_c + k, n_c), k)
        for k in range(1, n_c)
    ]
    gathered = [
        push(cols_ref, cols_land.at[me_e], "exp", lax.rem(me_e + k, n_e), 2 * n_c + k)
        for k in range(1, n_e)
    ]
    parts_land[me_c] = parts_ref[me_c]
    cols_land[me_e] = cols_ref[...]
    for copy in scattered:
        copy.wait()
    chunk[...] = jnp.sum(parts_land[...], axis=0)
    chunk_land[me_c] = chunk[...]
    spread = [
        push(chunk, chunk_land.at[me_c], "ctx", lax.rem(me_c + k, n_c), n_c + k)
        for k in range(1, n_c)
    ]
    for copy in gathered + spread:
        copy.wait()
    cols_out[...] = cols_land[...]
    rate_out[...] = chunk_land[...]


def reduce_partials(cols, parts, collective_id):
    n_e, n_c = lax.axis_size("exp"), lax.axis_size("ctx")
    return pl.pallas_call(
        reduce_kernel,
        out_shape=(
            jax.ShapeDtypeStruct((n_e,) + cols.shape, cols.dtype),
            jax.ShapeDtypeStruct(parts.shape, parts.dtype),
        ),
        scratch_shapes=[
            pltpu.VMEM((n_e,) + cols.shape, cols.dtype),
            pltpu.VMEM(parts.shape, parts.dtype),
            pltpu.VMEM(parts.shape[1:], parts.dtype),
            pltpu.VMEM(parts.shape, parts.dtype),
            pltpu.SemaphoreType.DMA((2, 2 * n_c + n_e)),
        ],
        compiler_params=pltpu.CompilerParams(collective_id=collective_id, has_side_effects=True),
    )(cols, parts)


def slot_buffer(moe_grad, route, gate_prob, capacity):
    pair_count = route.shape[0] * route.shape[1]
    weighted = (gate_prob[:, :, None] * moe_grad.astype(jnp.float32)[:, None, :]).astype(
        jnp.bfloat16
    )
    weighted = weighted.reshape(pair_count, moe_grad.shape[1])
    flat_route = route.reshape(pair_count)
    onehot = (flat_route[:, None] == jnp.arange(EXPERTS, dtype=jnp.int32)[None, :]).astype(
        jnp.int32
    )
    ranks = jnp.sum((jnp.cumsum(onehot, axis=0) - onehot) * onehot, axis=1)
    target = flat_route * capacity + ranks
    placing = (target[:, None] == jnp.arange(EXPERTS * capacity, dtype=jnp.int32)[None, :]).astype(
        jnp.bfloat16
    )
    buffer = jnp.einsum("ps,pd->sd", placing, weighted, preferred_element_type=jnp.float32).astype(
        jnp.bfloat16
    )
    return buffer.reshape(EXPERTS, capacity, moe_grad.shape[1])


def body(
    scan_input,
    step_size,
    decay_rate,
    input_proj,
    output_proj,
    skip_gain,
    block_states,
    end_grad,
    scan_grad,
    moe_grad,
    route,
    gate_prob,
    w_down,
    hidden_saved,
):
    inputs = scan_input.astype(jnp.float32)
    steps = step_size.astype(jnp.float32)
    grads = scan_grad.astype(jnp.float32)
    bmats = input_proj.T
    cmats = output_proj.T
    first_state = block_states[0]
    decays = jnp.exp(-steps[:, None, :] * decay_rate[None])
    driving = (steps * inputs)[:, None, :] * bmats[:, :, None]
    sources = cmats[:, :, None] * grads[:, None, :]
    states, seed = local_scans(decays, driving, sources, first_state)
    before = jnp.concatenate([first_state[None], states[:-1]], axis=0)
    out_cols = jnp.sum(states * grads[:, None, :], axis=2)
    shrink = jnp.exp(-decay_rate * jnp.sum(steps, axis=0)[None])
    position = lax.axis_index("ctx")
    count = lax.axis_size("ctx")
    is_last = position == count - 1
    pair = jnp.stack(
        [jnp.where(is_last, 0.0, shrink), jnp.where(is_last, shrink * end_grad + seed, seed)]
    )
    slot_total = hidden_saved.shape[1]
    capacity = slot_total // (lax.axis_size("ctx") * lax.axis_size("exp"))
    buffer = slot_buffer(moe_grad, route, gate_prob, capacity)
    received_rows = lax.all_to_all(buffer, "exp", split_axis=0, concat_axis=1, tiled=True)
    relayed, all_rows = relay(pair, received_rows, "ctx", 4)
    entering = jnp.where(is_last, end_grad, relayed)
    adjoint = adjoint_scan(decays, sources, entering)
    input_grad = (
        steps * jnp.sum(bmats[:, :, None] * adjoint, axis=1) + skip_gain[None] * grads
    ).astype(jnp.bfloat16)
    step_grad = jnp.sum(
        adjoint * (bmats[:, :, None] * inputs[:, None, :] - decay_rate[None] * decays * before),
        axis=1,
    ).astype(jnp.bfloat16)
    in_cols = jnp.sum(adjoint * (steps * inputs)[:, None, :], axis=2)
    rate_local = jnp.sum(adjoint * (-steps[:, None, :] * decays * before), axis=0)
    ctx_count = lax.axis_size("ctx")
    rate_parts = rate_local.reshape(ctx_count, 1, rate_local.size // ctx_count)
    col_parts, rate_chunks = reduce_partials(jnp.stack([in_cols.T, out_cols.T]), rate_parts, 1)
    col_sums = jnp.sum(col_parts, axis=0)
    in_proj_grad, out_proj_grad = col_sums[0], col_sums[1]
    decay_grad = rate_chunks.reshape(rate_local.shape)
    weight_total = jnp.einsum(
        "lrf,lrd->lfd", hidden_saved, all_rows, preferred_element_type=jnp.float32
    )
    hidden_grad = jnp.einsum(
        "lrd,lfd->lrf", all_rows, w_down, preferred_element_type=jnp.float32
    ).astype(jnp.bfloat16)
    down_grad = weight_total.astype(jnp.bfloat16)
    return (input_grad, step_grad, in_proj_grad, out_proj_grad, decay_grad, down_grad, hidden_grad)


def solution(mesh):
    placed = (
        P("ctx", "exp"),
        P("ctx", "exp"),
        P(None, "exp"),
        P(None, "ctx"),
        P(None, "ctx"),
        P("exp"),
        P("ctx", None, "exp"),
        P(None, "exp"),
        P("ctx", "exp"),
        P(("ctx", "exp"), None),
        P(("ctx", "exp"), None),
        P(("ctx", "exp"), None),
        P("exp", "ctx", None),
        P("exp", None, "ctx"),
    )
    return jax.shard_map(
        body,
        mesh=mesh,
        in_specs=placed,
        out_specs=(
            P("ctx", "exp"),
            P("ctx", "exp"),
            P(None, "ctx"),
            P(None, "ctx"),
            P(None, "exp"),
            P("exp", "ctx", None),
            P("exp", None, "ctx"),
        ),
        check_vma=False,
    )
```

```python
import functools

import jax
import jax.numpy as jnp
from jax import lax
from jax.experimental import pallas as pl
from jax.experimental.pallas import tpu as pltpu
from jax.sharding import PartitionSpec as P

EXPERTS = 16


def local_scans_kernel(decay_ref, drive_ref, source_ref, first_ref, states_ref, seed_ref):
    count = decay_ref.shape[0]

    def forward(t, state):
        state = decay_ref[t] * state + drive_ref[t]
        states_ref[t] = state
        return state

    lax.fori_loop(0, count, forward, first_ref[...], unroll=8)

    def backward(i, running):
        t = count - 1 - i
        return decay_ref[t] * (source_ref[t] + running)

    seed_ref[...] = lax.fori_loop(0, count, backward, jnp.zeros_like(first_ref[...]), unroll=8)


def local_scans(decays, driving, sources, first_state):
    return pl.pallas_call(
        local_scans_kernel,
        out_shape=(
            jax.ShapeDtypeStruct(decays.shape, jnp.float32),
            jax.ShapeDtypeStruct(first_state.shape, jnp.float32),
        ),
        cost_estimate=pl.CostEstimate(
            flops=4 * decays.size, bytes_accessed=16 * decays.size, transcendentals=0
        ),
    )(decays, driving, sources, first_state)


def adjoint_scan_kernel(decay_ref, source_ref, entering_ref, adjoint_ref):
    count = decay_ref.shape[0]

    def backward(i, running):
        t = count - 1 - i
        value = source_ref[t] + running
        adjoint_ref[t] = value
        return decay_ref[t] * value

    lax.fori_loop(0, count, backward, entering_ref[...], unroll=8)


def adjoint_scan(decays, sources, entering):
    return pl.pallas_call(
        adjoint_scan_kernel,
        out_shape=jax.ShapeDtypeStruct(decays.shape, jnp.float32),
        cost_estimate=pl.CostEstimate(
            flops=2 * decays.size, bytes_accessed=12 * decays.size, transcendentals=0
        ),
    )(decays, sources, entering)


def relay_kernel(axis, count, pair_ref, out_ref, held, land, send_sems, recv_sems):
    me = lax.axis_index(axis)
    distances = []
    while 1 << len(distances) < count:
        distances.append(1 << len(distances))
    land[...] = jnp.zeros_like(land)
    barrier = pltpu.get_barrier_semaphore()
    expected = 0
    for d in distances:

        @pl.when(me >= d)
        def _():
            pl.semaphore_signal(barrier, 1, device_id={axis: me - d}, device_id_type=pl.DeviceIdType.MESH)

        @pl.when(me + d < count)
        def _():
            pl.semaphore_signal(barrier, 1, device_id={axis: me + d}, device_id_type=pl.DeviceIdType.MESH)

        expected = expected + (me >= d).astype(jnp.int32) + (me + d < count).astype(jnp.int32)
    pl.semaphore_wait(barrier, expected)
    rounds = distances + [1]
    for r, d in enumerate(rounds):
        last_round = r == len(rounds) - 1
        source = pair_ref if r == 0 else held.at[r - 1]
        copy = pltpu.make_async_remote_copy(
            src_ref=source,
            dst_ref=land.at[r],
            send_sem=send_sems.at[r],
            recv_sem=recv_sems.at[r],
            device_id={axis: lax.rem(me - d + count, count)},
            device_id_type=pl.DeviceIdType.MESH,
        )

        @pl.when(me >= d)
        def _():
            copy.start()

        if not last_round:
            held[r] = source[...]

        @pl.when(me + d < count)
        def _():
            copy.wait_recv()
            if not last_round:
                shrink, seed = source[0], source[1]
                held[r, 0] = shrink * land[r, 0]
                held[r, 1] = shrink * land[r, 1] + seed

        @pl.when(me >= d)
        def _():
            copy.wait_send()

    out_ref[...] = land[len(rounds) - 1, 1]


def relay(pair, axis, collective_id):
    count = lax.axis_size(axis)
    rounds = max(1, (count - 1).bit_length()) + 1
    return pl.pallas_call(
        functools.partial(relay_kernel, axis, count),
        out_shape=jax.ShapeDtypeStruct(pair.shape[1:], pair.dtype),
        scratch_shapes=[
            pltpu.VMEM((rounds - 1,) + pair.shape, pair.dtype),
            pltpu.VMEM((rounds,) + pair.shape, pair.dtype),
            pltpu.SemaphoreType.DMA((rounds,)),
            pltpu.SemaphoreType.DMA((rounds,)),
        ],
        compiler_params=pltpu.CompilerParams(collective_id=collective_id, has_side_effects=True),
    )(pair)


def reduce_kernel(cols_ref, parts_ref, cols_out, rate_out, cols_land, parts_land, chunk, chunk_land, sems):
    me_e, me_c = lax.axis_index("exp"), lax.axis_index("ctx")
    n_e, n_c = lax.axis_size("exp"), lax.axis_size("ctx")
    mesh_id = pl.DeviceIdType.MESH
    barrier = pltpu.get_barrier_semaphore()
    for k in range(1, n_e):
        pl.semaphore_signal(barrier, 1, device_id={"exp": lax.rem(me_e + k, n_e)}, device_id_type=mesh_id)
    for k in range(1, n_c):
        pl.semaphore_signal(barrier, 1, device_id={"ctx": lax.rem(me_c + k, n_c)}, device_id_type=mesh_id)
    pl.semaphore_wait(barrier, n_e - 1 + n_c - 1)

    def push(src, dst, axis, peer, slot):
        copy = pltpu.make_async_remote_copy(
            src_ref=src,
            dst_ref=dst,
            send_sem=sems.at[0, slot],
            recv_sem=sems.at[1, slot],
            device_id={axis: peer},
            device_id_type=mesh_id,
        )
        copy.start()
        return copy

    scattered = [
        push(parts_ref.at[lax.rem(me_c + k, n_c)], parts_land.at[me_c], "ctx", lax.rem(me_c + k, n_c), k)
        for k in range(1, n_c)
    ]
    gathered = [
        push(cols_ref, cols_land.at[me_e], "exp", lax.rem(me_e + k, n_e), 2 * n_c + k)
        for k in range(1, n_e)
    ]
    parts_land[me_c] = parts_ref[me_c]
    cols_land[me_e] = cols_ref[...]
    for copy in scattered:
        copy.wait()
    chunk[...] = jnp.sum(parts_land[...], axis=0)
    chunk_land[me_c] = chunk[...]
    spread = [
        push(chunk, chunk_land.at[me_c], "ctx", lax.rem(me_c + k, n_c), n_c + k)
        for k in range(1, n_c)
    ]
    for copy in gathered + spread:
        copy.wait()
    cols_out[...] = cols_land[...]
    rate_out[...] = chunk_land[...]


def reduce_partials(cols, parts, collective_id):
    n_e, n_c = lax.axis_size("exp"), lax.axis_size("ctx")
    return pl.pallas_call(
        reduce_kernel,
        out_shape=(
            jax.ShapeDtypeStruct((n_e,) + cols.shape, cols.dtype),
            jax.ShapeDtypeStruct(parts.shape, parts.dtype),
        ),
        scratch_shapes=[
            pltpu.VMEM((n_e,) + cols.shape, cols.dtype),
            pltpu.VMEM(parts.shape, parts.dtype),
            pltpu.VMEM(parts.shape[1:], parts.dtype),
            pltpu.VMEM(parts.shape, parts.dtype),
            pltpu.SemaphoreType.DMA((2, 2 * n_c + n_e)),
        ],
        compiler_params=pltpu.CompilerParams(collective_id=collective_id, has_side_effects=True),
    )(cols, parts)


def slot_buffer(moe_grad, route, gate_prob, capacity):
    pair_count = route.shape[0] * route.shape[1]
    weighted = (gate_prob[:, :, None] * moe_grad.astype(jnp.float32)[:, None, :]).astype(
        jnp.bfloat16
    )
    weighted = weighted.reshape(pair_count, moe_grad.shape[1])
    flat_route = route.reshape(pair_count)
    onehot = (flat_route[:, None] == jnp.arange(EXPERTS, dtype=jnp.int32)[None, :]).astype(
        jnp.int32
    )
    ranks = jnp.sum((jnp.cumsum(onehot, axis=0) - onehot) * onehot, axis=1)
    target = flat_route * capacity + ranks
    placing = (target[:, None] == jnp.arange(EXPERTS * capacity, dtype=jnp.int32)[None, :]).astype(
        jnp.bfloat16
    )
    buffer = jnp.einsum("ps,pd->sd", placing, weighted, preferred_element_type=jnp.float32).astype(
        jnp.bfloat16
    )
    return buffer.reshape(EXPERTS, capacity, moe_grad.shape[1])


def body(
    scan_input,
    step_size,
    decay_rate,
    input_proj,
    output_proj,
    skip_gain,
    block_states,
    end_grad,
    scan_grad,
    moe_grad,
    route,
    gate_prob,
    w_down,
    hidden_saved,
):
    inputs = scan_input.astype(jnp.float32)
    steps = step_size.astype(jnp.float32)
    grads = scan_grad.astype(jnp.float32)
    bmats = input_proj.T
    cmats = output_proj.T
    first_state = block_states[0]
    decays = jnp.exp(-steps[:, None, :] * decay_rate[None])
    driving = (steps * inputs)[:, None, :] * bmats[:, :, None]
    sources = cmats[:, :, None] * grads[:, None, :]
    states, seed = local_scans(decays, driving, sources, first_state)
    before = jnp.concatenate([first_state[None], states[:-1]], axis=0)
    out_cols = jnp.sum(states * grads[:, None, :], axis=2)
    shrink = jnp.exp(-decay_rate * jnp.sum(steps, axis=0)[None])
    position = lax.axis_index("ctx")
    count = lax.axis_size("ctx")
    is_last = position == count - 1
    pair = jnp.stack(
        [jnp.where(is_last, 0.0, shrink), jnp.where(is_last, shrink * end_grad + seed, seed)]
    )
    entering = jnp.where(is_last, end_grad, relay(pair, "ctx", 4))
    adjoint = adjoint_scan(decays, sources, entering)
    input_grad = (
        steps * jnp.sum(bmats[:, :, None] * adjoint, axis=1) + skip_gain[None] * grads
    ).astype(jnp.bfloat16)
    step_grad = jnp.sum(
        adjoint * (bmats[:, :, None] * inputs[:, None, :] - decay_rate[None] * decays * before),
        axis=1,
    ).astype(jnp.bfloat16)
    in_cols = jnp.sum(adjoint * (steps * inputs)[:, None, :], axis=2)
    rate_local = jnp.sum(adjoint * (-steps[:, None, :] * decays * before), axis=0)
    ctx_count = lax.axis_size("ctx")
    rate_parts = rate_local.reshape(ctx_count, 1, rate_local.size // ctx_count)
    col_parts, rate_chunks = reduce_partials(jnp.stack([in_cols.T, out_cols.T]), rate_parts, 1)
    col_sums = jnp.sum(col_parts, axis=0)
    in_proj_grad, out_proj_grad = col_sums[0], col_sums[1]
    decay_grad = rate_chunks.reshape(rate_local.shape)
    slot_total = hidden_saved.shape[1]
    capacity = slot_total // (lax.axis_size("ctx") * lax.axis_size("exp"))
    buffer = slot_buffer(moe_grad, route, gate_prob, capacity)
    received_rows = lax.all_to_all(buffer, "exp", split_axis=0, concat_axis=1, tiled=True)
    half = received_rows.shape[2] // 2
    row_halves = [
        lax.all_gather(received_rows[:, :, :half], "ctx", axis=1, tiled=True),
        lax.all_gather(received_rows[:, :, half:], "ctx", axis=1, tiled=True),
    ]
    down_grad = jnp.concatenate(
        [
            jnp.einsum("lrf,lrd->lfd", hidden_saved, rows, preferred_element_type=jnp.float32)
            for rows in row_halves
        ],
        axis=2,
    ).astype(jnp.bfloat16)
    hidden_grad = (
        jnp.einsum(
            "lrd,lfd->lrf", row_halves[0], w_down[:, :, :half], preferred_element_type=jnp.float32
        )
        + jnp.einsum(
            "lrd,lfd->lrf", row_halves[1], w_down[:, :, half:], preferred_element_type=jnp.float32
        )
    ).astype(jnp.bfloat16)
    return (input_grad, step_grad, in_proj_grad, out_proj_grad, decay_grad, down_grad, hidden_grad)


def solution(mesh):
    placed = (
        P("ctx", "exp"),
        P("ctx", "exp"),
        P(None, "exp"),
        P(None, "ctx"),
        P(None, "ctx"),
        P("exp"),
        P("ctx", None, "exp"),
        P(None, "exp"),
        P("ctx", "exp"),
        P(("ctx", "exp"), None),
        P(("ctx", "exp"), None),
        P(("ctx", "exp"), None),
        P("exp", "ctx", None),
        P("exp", None, "ctx"),
    )
    return jax.shard_map(
        body,
        mesh=mesh,
        in_specs=placed,
        out_specs=(
            P("ctx", "exp"),
            P("ctx", "exp"),
            P(None, "ctx"),
            P(None, "ctx"),
            P(None, "exp"),
            P("exp", "ctx", None),
            P("exp", None, "ctx"),
        ),
        check_vma=False,
    )
```

```python
import functools

import jax
import jax.numpy as jnp
from jax import lax
from jax.experimental import pallas as pl
from jax.experimental.pallas import tpu as pltpu
from jax.sharding import PartitionSpec as P

EXPERTS = 16


def local_scans_kernel(decay_ref, drive_ref, source_ref, first_ref, states_ref, before_ref, seed_ref):
    count = decay_ref.shape[0]

    def forward(t, state):
        before_ref[t] = state
        state = decay_ref[t] * state + drive_ref[t]
        states_ref[t] = state
        return state

    lax.fori_loop(0, count, forward, first_ref[...], unroll=8)

    def backward(i, running):
        t = count - 1 - i
        return decay_ref[t] * (source_ref[t] + running)

    seed_ref[...] = lax.fori_loop(0, count, backward, jnp.zeros_like(first_ref[...]), unroll=8)


def local_scans(decays, driving, sources, first_state):
    return pl.pallas_call(
        local_scans_kernel,
        out_shape=(
            jax.ShapeDtypeStruct(decays.shape, jnp.float32),
            jax.ShapeDtypeStruct(decays.shape, jnp.float32),
            jax.ShapeDtypeStruct(first_state.shape, jnp.float32),
        ),
        cost_estimate=pl.CostEstimate(
            flops=4 * decays.size, bytes_accessed=20 * decays.size, transcendentals=0
        ),
    )(decays, driving, sources, first_state)


def adjoint_scan_kernel(decay_ref, source_ref, entering_ref, adjoint_ref):
    count = decay_ref.shape[0]

    def backward(i, running):
        t = count - 1 - i
        value = source_ref[t] + running
        adjoint_ref[t] = value
        return decay_ref[t] * value

    lax.fori_loop(0, count, backward, entering_ref[...], unroll=8)


def adjoint_scan(decays, sources, entering):
    return pl.pallas_call(
        adjoint_scan_kernel,
        out_shape=jax.ShapeDtypeStruct(decays.shape, jnp.float32),
        cost_estimate=pl.CostEstimate(
            flops=2 * decays.size, bytes_accessed=12 * decays.size, transcendentals=0
        ),
    )(decays, sources, entering)


def relay_kernel(axis, count, pair_ref, out_ref, held, land, send_sems, recv_sems):
    me = lax.axis_index(axis)
    distances = []
    while 1 << len(distances) < count:
        distances.append(1 << len(distances))
    land[...] = jnp.zeros_like(land)
    barrier = pltpu.get_barrier_semaphore()
    expected = 0
    for d in distances:

        @pl.when(me >= d)
        def _():
            pl.semaphore_signal(barrier, 1, device_id={axis: me - d}, device_id_type=pl.DeviceIdType.MESH)

        @pl.when(me + d < count)
        def _():
            pl.semaphore_signal(barrier, 1, device_id={axis: me + d}, device_id_type=pl.DeviceIdType.MESH)

        expected = expected + (me >= d).astype(jnp.int32) + (me + d < count).astype(jnp.int32)
    pl.semaphore_wait(barrier, expected)
    rounds = distances + [1]
    for r, d in enumerate(rounds):
        last_round = r == len(rounds) - 1
        source = pair_ref if r == 0 else held.at[r - 1]
        copy = pltpu.make_async_remote_copy(
            src_ref=source,
            dst_ref=land.at[r],
            send_sem=send_sems.at[r],
            recv_sem=recv_sems.at[r],
            device_id={axis: lax.rem(me - d + count, count)},
            device_id_type=pl.DeviceIdType.MESH,
        )

        @pl.when(me >= d)
        def _():
            copy.start()

        if not last_round:
            held[r] = source[...]

        @pl.when(me + d < count)
        def _():
            copy.wait_recv()
            if not last_round:
                shrink, seed = source[0], source[1]
                held[r, 0] = shrink * land[r, 0]
                held[r, 1] = shrink * land[r, 1] + seed

        @pl.when(me >= d)
        def _():
            copy.wait_send()

    out_ref[...] = land[len(rounds) - 1, 1]


def relay(pair, axis, collective_id):
    count = lax.axis_size(axis)
    rounds = max(1, (count - 1).bit_length()) + 1
    return pl.pallas_call(
        functools.partial(relay_kernel, axis, count),
        out_shape=jax.ShapeDtypeStruct(pair.shape[1:], pair.dtype),
        scratch_shapes=[
            pltpu.VMEM((rounds - 1,) + pair.shape, pair.dtype),
            pltpu.VMEM((rounds,) + pair.shape, pair.dtype),
            pltpu.SemaphoreType.DMA((rounds,)),
            pltpu.SemaphoreType.DMA((rounds,)),
        ],
        compiler_params=pltpu.CompilerParams(collective_id=collective_id, has_side_effects=True),
    )(pair)


def reduce_kernel(cols_ref, parts_ref, cols_out, rate_out, cols_land, parts_land, chunk, chunk_land, sems):
    me_e, me_c = lax.axis_index("exp"), lax.axis_index("ctx")
    n_e, n_c = lax.axis_size("exp"), lax.axis_size("ctx")
    mesh_id = pl.DeviceIdType.MESH
    barrier = pltpu.get_barrier_semaphore()
    for k in range(1, n_e):
        pl.semaphore_signal(barrier, 1, device_id={"exp": lax.rem(me_e + k, n_e)}, device_id_type=mesh_id)
    for k in range(1, n_c):
        pl.semaphore_signal(barrier, 1, device_id={"ctx": lax.rem(me_c + k, n_c)}, device_id_type=mesh_id)
    pl.semaphore_wait(barrier, n_e - 1 + n_c - 1)

    def push(src, dst, axis, peer, slot):
        copy = pltpu.make_async_remote_copy(
            src_ref=src,
            dst_ref=dst,
            send_sem=sems.at[0, slot],
            recv_sem=sems.at[1, slot],
            device_id={axis: peer},
            device_id_type=mesh_id,
        )
        copy.start()
        return copy

    scattered = [
        push(parts_ref.at[lax.rem(me_c + k, n_c)], parts_land.at[me_c], "ctx", lax.rem(me_c + k, n_c), k)
        for k in range(1, n_c)
    ]
    gathered = [
        push(cols_ref, cols_land.at[me_e], "exp", lax.rem(me_e + k, n_e), 2 * n_c + k)
        for k in range(1, n_e)
    ]
    parts_land[me_c] = parts_ref[me_c]
    cols_land[me_e] = cols_ref[...]
    for copy in scattered:
        copy.wait()
    chunk[...] = jnp.sum(parts_land[...], axis=0)
    chunk_land[me_c] = chunk[...]
    spread = [
        push(chunk, chunk_land.at[me_c], "ctx", lax.rem(me_c + k, n_c), n_c + k)
        for k in range(1, n_c)
    ]
    for copy in gathered + spread:
        copy.wait()
    cols_out[...] = cols_land[...]
    rate_out[...] = chunk_land[...]


def reduce_partials(cols, parts, collective_id):
    n_e, n_c = lax.axis_size("exp"), lax.axis_size("ctx")
    return pl.pallas_call(
        reduce_kernel,
        out_shape=(
            jax.ShapeDtypeStruct((n_e,) + cols.shape, cols.dtype),
            jax.ShapeDtypeStruct(parts.shape, parts.dtype),
        ),
        scratch_shapes=[
            pltpu.VMEM((n_e,) + cols.shape, cols.dtype),
            pltpu.VMEM(parts.shape, parts.dtype),
            pltpu.VMEM(parts.shape[1:], parts.dtype),
            pltpu.VMEM(parts.shape, parts.dtype),
            pltpu.SemaphoreType.DMA((2, 2 * n_c + n_e)),
        ],
        compiler_params=pltpu.CompilerParams(collective_id=collective_id, has_side_effects=True),
    )(cols, parts)


def slot_buffer(moe_grad, route, gate_prob, capacity):
    pair_count = route.shape[0] * route.shape[1]
    weighted = (gate_prob[:, :, None] * moe_grad.astype(jnp.float32)[:, None, :]).astype(
        jnp.bfloat16
    )
    weighted = weighted.reshape(pair_count, moe_grad.shape[1])
    flat_route = route.reshape(pair_count)
    onehot = (flat_route[:, None] == jnp.arange(EXPERTS, dtype=jnp.int32)[None, :]).astype(
        jnp.int32
    )
    ranks = jnp.sum((jnp.cumsum(onehot, axis=0) - onehot) * onehot, axis=1)
    target = flat_route * capacity + ranks
    placing = (target[:, None] == jnp.arange(EXPERTS * capacity, dtype=jnp.int32)[None, :]).astype(
        jnp.bfloat16
    )
    buffer = jnp.einsum("ps,pd->sd", placing, weighted, preferred_element_type=jnp.float32).astype(
        jnp.bfloat16
    )
    return buffer.reshape(EXPERTS, capacity, moe_grad.shape[1])


def body(
    scan_input,
    step_size,
    decay_rate,
    input_proj,
    output_proj,
    skip_gain,
    block_states,
    end_grad,
    scan_grad,
    moe_grad,
    route,
    gate_prob,
    w_down,
    hidden_saved,
):
    inputs = scan_input.astype(jnp.float32)
    steps = step_size.astype(jnp.float32)
    grads = scan_grad.astype(jnp.float32)
    bmats = input_proj.T
    cmats = output_proj.T
    first_state = block_states[0]
    decays = jnp.exp(-steps[:, None, :] * decay_rate[None])
    driving = (steps * inputs)[:, None, :] * bmats[:, :, None]
    sources = cmats[:, :, None] * grads[:, None, :]
    states, before, seed = local_scans(decays, driving, sources, first_state)
    out_cols = jnp.sum(states * grads[:, None, :], axis=2)
    shrink = jnp.exp(-decay_rate * jnp.sum(steps, axis=0)[None])
    position = lax.axis_index("ctx")
    count = lax.axis_size("ctx")
    is_last = position == count - 1
    pair = jnp.stack(
        [jnp.where(is_last, 0.0, shrink), jnp.where(is_last, shrink * end_grad + seed, seed)]
    )
    entering = jnp.where(is_last, end_grad, relay(pair, "ctx", 4))
    adjoint = adjoint_scan(decays, sources, entering)
    input_grad = (
        steps * jnp.sum(bmats[:, :, None] * adjoint, axis=1) + skip_gain[None] * grads
    ).astype(jnp.bfloat16)
    step_grad = jnp.sum(
        adjoint * (bmats[:, :, None] * inputs[:, None, :] - decay_rate[None] * decays * before),
        axis=1,
    ).astype(jnp.bfloat16)
    in_cols = jnp.sum(adjoint * (steps * inputs)[:, None, :], axis=2)
    rate_local = jnp.sum(adjoint * (-steps[:, None, :] * decays * before), axis=0)
    ctx_count = lax.axis_size("ctx")
    rate_parts = rate_local.reshape(ctx_count, 1, rate_local.size // ctx_count)
    col_parts, rate_chunks = reduce_partials(jnp.stack([in_cols.T, out_cols.T]), rate_parts, 1)
    col_sums = jnp.sum(col_parts, axis=0)
    in_proj_grad, out_proj_grad = col_sums[0], col_sums[1]
    decay_grad = rate_chunks.reshape(rate_local.shape)
    slot_total = hidden_saved.shape[1]
    capacity = slot_total // (lax.axis_size("ctx") * lax.axis_size("exp"))
    buffer = slot_buffer(moe_grad, route, gate_prob, capacity)
    received_rows = lax.all_to_all(buffer, "exp", split_axis=0, concat_axis=1, tiled=True)
    all_rows = lax.all_gather(received_rows, "ctx", axis=1, tiled=True)
    weight_total = jnp.einsum(
        "lrf,lrd->lfd", hidden_saved, all_rows, preferred_element_type=jnp.float32
    )
    hidden_grad = jnp.einsum(
        "lrd,lfd->lrf", all_rows, w_down, preferred_element_type=jnp.float32
    ).astype(jnp.bfloat16)
    down_grad = weight_total.astype(jnp.bfloat16)
    return (input_grad, step_grad, in_proj_grad, out_proj_grad, decay_grad, down_grad, hidden_grad)


def solution(mesh):
    placed = (
        P("ctx", "exp"),
        P("ctx", "exp"),
        P(None, "exp"),
        P(None, "ctx"),
        P(None, "ctx"),
        P("exp"),
        P("ctx", None, "exp"),
        P(None, "exp"),
        P("ctx", "exp"),
        P(("ctx", "exp"), None),
        P(("ctx", "exp"), None),
        P(("ctx", "exp"), None),
        P("exp", "ctx", None),
        P("exp", None, "ctx"),
    )
    return jax.shard_map(
        body,
        mesh=mesh,
        in_specs=placed,
        out_specs=(
            P("ctx", "exp"),
            P("ctx", "exp"),
            P(None, "ctx"),
            P(None, "ctx"),
            P(None, "exp"),
            P("exp", "ctx", None),
            P("exp", None, "ctx"),
        ),
        check_vma=False,
    )
```

```python
import functools

import jax
import jax.numpy as jnp
from jax import lax
from jax.experimental import pallas as pl
from jax.experimental.pallas import tpu as pltpu
from jax.sharding import PartitionSpec as P

EXPERTS = 16


def local_scans_kernel(decay_ref, drive_ref, source_ref, first_ref, states_ref, before_ref, seed_ref):
    count = decay_ref.shape[0]

    def forward(t, state):
        before_ref[t] = state
        state = decay_ref[t] * state + drive_ref[t]
        states_ref[t] = state
        return state

    lax.fori_loop(0, count, forward, first_ref[...], unroll=8)

    def backward(i, running):
        t = count - 1 - i
        return decay_ref[t] * (source_ref[t] + running)

    seed_ref[...] = lax.fori_loop(0, count, backward, jnp.zeros_like(first_ref[...]), unroll=8)


def local_scans(decays, driving, sources, first_state):
    return pl.pallas_call(
        local_scans_kernel,
        out_shape=(
            jax.ShapeDtypeStruct(decays.shape, jnp.float32),
            jax.ShapeDtypeStruct(decays.shape, jnp.float32),
            jax.ShapeDtypeStruct(first_state.shape, jnp.float32),
        ),
        cost_estimate=pl.CostEstimate(
            flops=4 * decays.size, bytes_accessed=20 * decays.size, transcendentals=0
        ),
    )(decays, driving, sources, first_state)


def adjoint_scan_kernel(decay_ref, source_ref, entering_ref, adjoint_ref):
    count = decay_ref.shape[0]

    def backward(i, running):
        t = count - 1 - i
        value = source_ref[t] + running
        adjoint_ref[t] = value
        return decay_ref[t] * value

    lax.fori_loop(0, count, backward, entering_ref[...], unroll=8)


def adjoint_scan(decays, sources, entering):
    return pl.pallas_call(
        adjoint_scan_kernel,
        out_shape=jax.ShapeDtypeStruct(decays.shape, jnp.float32),
        cost_estimate=pl.CostEstimate(
            flops=2 * decays.size, bytes_accessed=12 * decays.size, transcendentals=0
        ),
    )(decays, sources, entering)


def adjoint_full_kernel(
    decay_ref, source_ref, entering_ref, bmat_ref, inp_ref, step_ref, grad_ref, before_ref,
    rate_ref, skip_ref, input_out, step_out, in_cols_out, rate_out, adjoint_ref,
):
    count = decay_ref.shape[0]

    def backward(i, running):
        t = count - 1 - i
        value = source_ref[t] + running
        adjoint_ref[t] = value
        return decay_ref[t] * value

    lax.fori_loop(0, count, backward, entering_ref[...], unroll=8)
    width = 16

    def reduce(c, total):
        ts = pl.ds(pl.multiple_of(c * width, width), width)
        adj, bcol = adjoint_ref[ts], bmat_ref[ts]
        inp, stp, grad = inp_ref[ts], step_ref[ts], grad_ref[ts]
        dec, bef = decay_ref[ts], before_ref[ts]
        input_out[ts] = (
            stp * jnp.sum(bcol * adj, axis=1) + skip_ref[...] * grad
        ).astype(input_out.dtype)
        step_out[ts] = jnp.sum(
            adj * (bcol * inp[:, None, :] - rate_ref[...][None] * dec * bef), axis=1
        ).astype(step_out.dtype)
        in_cols_out[ts] = jnp.sum(adj * (stp * inp)[:, None, :], axis=2)
        return total + jnp.sum(adj * (-stp[:, None, :] * dec * bef), axis=0)

    rate_out[...] = lax.fori_loop(0, count // width, reduce, jnp.zeros_like(rate_ref[...]))


def adjoint_full(decays, sources, entering, bmats, inputs, steps, grads, before, rate, skip):
    count, states, width = decays.shape
    return pl.pallas_call(
        adjoint_full_kernel,
        out_shape=(
            jax.ShapeDtypeStruct((count, width), jnp.bfloat16),
            jax.ShapeDtypeStruct((count, width), jnp.bfloat16),
            jax.ShapeDtypeStruct((count, states), jnp.float32),
            jax.ShapeDtypeStruct((states, width), jnp.float32),
        ),
        scratch_shapes=[pltpu.VMEM(decays.shape, jnp.float32)],
        cost_estimate=pl.CostEstimate(
            flops=16 * decays.size, bytes_accessed=12 * decays.size, transcendentals=0
        ),
    )(decays, sources, entering, bmats[:, :, None], inputs, steps, grads, before, rate, skip[None])


def relay_kernel(axis, count, pair_ref, out_ref, held, land, send_sems, recv_sems):
    me = lax.axis_index(axis)
    distances = []
    while 1 << len(distances) < count:
        distances.append(1 << len(distances))
    land[...] = jnp.zeros_like(land)
    barrier = pltpu.get_barrier_semaphore()
    expected = 0
    for d in distances:

        @pl.when(me >= d)
        def _():
            pl.semaphore_signal(barrier, 1, device_id={axis: me - d}, device_id_type=pl.DeviceIdType.MESH)

        @pl.when(me + d < count)
        def _():
            pl.semaphore_signal(barrier, 1, device_id={axis: me + d}, device_id_type=pl.DeviceIdType.MESH)

        expected = expected + (me >= d).astype(jnp.int32) + (me + d < count).astype(jnp.int32)
    pl.semaphore_wait(barrier, expected)
    rounds = distances + [1]
    for r, d in enumerate(rounds):
        last_round = r == len(rounds) - 1
        source = pair_ref if r == 0 else held.at[r - 1]
        copy = pltpu.make_async_remote_copy(
            src_ref=source,
            dst_ref=land.at[r],
            send_sem=send_sems.at[r],
            recv_sem=recv_sems.at[r],
            device_id={axis: lax.rem(me - d + count, count)},
            device_id_type=pl.DeviceIdType.MESH,
        )

        @pl.when(me >= d)
        def _():
            copy.start()

        if not last_round:
            held[r] = source[...]

        @pl.when(me + d < count)
        def _():
            copy.wait_recv()
            if not last_round:
                shrink, seed = source[0], source[1]
                held[r, 0] = shrink * land[r, 0]
                held[r, 1] = shrink * land[r, 1] + seed

        @pl.when(me >= d)
        def _():
            copy.wait_send()

    out_ref[...] = land[len(rounds) - 1, 1]


def relay(pair, axis, collective_id):
    count = lax.axis_size(axis)
    rounds = max(1, (count - 1).bit_length()) + 1
    return pl.pallas_call(
        functools.partial(relay_kernel, axis, count),
        out_shape=jax.ShapeDtypeStruct(pair.shape[1:], pair.dtype),
        scratch_shapes=[
            pltpu.VMEM((rounds - 1,) + pair.shape, pair.dtype),
            pltpu.VMEM((rounds,) + pair.shape, pair.dtype),
            pltpu.SemaphoreType.DMA((rounds,)),
            pltpu.SemaphoreType.DMA((rounds,)),
        ],
        compiler_params=pltpu.CompilerParams(collective_id=collective_id, has_side_effects=True),
    )(pair)


def reduce_kernel(cols_ref, parts_ref, cols_out, rate_out, cols_land, parts_land, chunk, chunk_land, sems):
    me_e, me_c = lax.axis_index("exp"), lax.axis_index("ctx")
    n_e, n_c = lax.axis_size("exp"), lax.axis_size("ctx")
    mesh_id = pl.DeviceIdType.MESH
    barrier = pltpu.get_barrier_semaphore()
    for k in range(1, n_e):
        pl.semaphore_signal(barrier, 1, device_id={"exp": lax.rem(me_e + k, n_e)}, device_id_type=mesh_id)
    for k in range(1, n_c):
        pl.semaphore_signal(barrier, 1, device_id={"ctx": lax.rem(me_c + k, n_c)}, device_id_type=mesh_id)
    pl.semaphore_wait(barrier, n_e - 1 + n_c - 1)

    def push(src, dst, axis, peer, slot):
        copy = pltpu.make_async_remote_copy(
            src_ref=src,
            dst_ref=dst,
            send_sem=sems.at[0, slot],
            recv_sem=sems.at[1, slot],
            device_id={axis: peer},
            device_id_type=mesh_id,
        )
        copy.start()
        return copy

    scattered = [
        push(parts_ref.at[lax.rem(me_c + k, n_c)], parts_land.at[me_c], "ctx", lax.rem(me_c + k, n_c), k)
        for k in range(1, n_c)
    ]
    gathered = [
        push(cols_ref, cols_land.at[me_e], "exp", lax.rem(me_e + k, n_e), 2 * n_c + k)
        for k in range(1, n_e)
    ]
    parts_land[me_c] = parts_ref[me_c]
    cols_land[me_e] = cols_ref[...]
    for copy in scattered:
        copy.wait()
    chunk[...] = jnp.sum(parts_land[...], axis=0)
    chunk_land[me_c] = chunk[...]
    spread = [
        push(chunk, chunk_land.at[me_c], "ctx", lax.rem(me_c + k, n_c), n_c + k)
        for k in range(1, n_c)
    ]
    for copy in gathered + spread:
        copy.wait()
    cols_out[...] = cols_land[...]
    rate_out[...] = chunk_land[...]


def reduce_partials(cols, parts, collective_id):
    n_e, n_c = lax.axis_size("exp"), lax.axis_size("ctx")
    return pl.pallas_call(
        reduce_kernel,
        out_shape=(
            jax.ShapeDtypeStruct((n_e,) + cols.shape, cols.dtype),
            jax.ShapeDtypeStruct(parts.shape, parts.dtype),
        ),
        scratch_shapes=[
            pltpu.VMEM((n_e,) + cols.shape, cols.dtype),
            pltpu.VMEM(parts.shape, parts.dtype),
            pltpu.VMEM(parts.shape[1:], parts.dtype),
            pltpu.VMEM(parts.shape, parts.dtype),
            pltpu.SemaphoreType.DMA((2, 2 * n_c + n_e)),
        ],
        compiler_params=pltpu.CompilerParams(collective_id=collective_id, has_side_effects=True),
    )(cols, parts)


def slot_buffer(moe_grad, route, gate_prob, capacity):
    pair_count = route.shape[0] * route.shape[1]
    weighted = (gate_prob[:, :, None] * moe_grad.astype(jnp.float32)[:, None, :]).astype(
        jnp.bfloat16
    )
    weighted = weighted.reshape(pair_count, moe_grad.shape[1])
    flat_route = route.reshape(pair_count)
    onehot = (flat_route[:, None] == jnp.arange(EXPERTS, dtype=jnp.int32)[None, :]).astype(
        jnp.int32
    )
    ranks = jnp.sum((jnp.cumsum(onehot, axis=0) - onehot) * onehot, axis=1)
    target = flat_route * capacity + ranks
    placing = (target[:, None] == jnp.arange(EXPERTS * capacity, dtype=jnp.int32)[None, :]).astype(
        jnp.bfloat16
    )
    buffer = jnp.einsum("ps,pd->sd", placing, weighted, preferred_element_type=jnp.float32).astype(
        jnp.bfloat16
    )
    return buffer.reshape(EXPERTS, capacity, moe_grad.shape[1])


def body(
    scan_input,
    step_size,
    decay_rate,
    input_proj,
    output_proj,
    skip_gain,
    block_states,
    end_grad,
    scan_grad,
    moe_grad,
    route,
    gate_prob,
    w_down,
    hidden_saved,
):
    inputs = scan_input.astype(jnp.float32)
    steps = step_size.astype(jnp.float32)
    grads = scan_grad.astype(jnp.float32)
    bmats = input_proj.T
    cmats = output_proj.T
    first_state = block_states[0]
    decays = jnp.exp(-steps[:, None, :] * decay_rate[None])
    driving = (steps * inputs)[:, None, :] * bmats[:, :, None]
    sources = cmats[:, :, None] * grads[:, None, :]
    states, before, seed = local_scans(decays, driving, sources, first_state)
    out_cols = jnp.sum(states * grads[:, None, :], axis=2)
    shrink = jnp.exp(-decay_rate * jnp.sum(steps, axis=0)[None])
    position = lax.axis_index("ctx")
    count = lax.axis_size("ctx")
    is_last = position == count - 1
    pair = jnp.stack(
        [jnp.where(is_last, 0.0, shrink), jnp.where(is_last, shrink * end_grad + seed, seed)]
    )
    entering = jnp.where(is_last, end_grad, relay(pair, "ctx", 4))
    input_grad, step_grad, in_cols, rate_local = adjoint_full(
        decays, sources, entering, bmats, inputs, steps, grads, before, decay_rate, skip_gain
    )
    ctx_count = lax.axis_size("ctx")
    rate_parts = rate_local.reshape(ctx_count, 1, rate_local.size // ctx_count)
    col_parts, rate_chunks = reduce_partials(jnp.stack([in_cols.T, out_cols.T]), rate_parts, 1)
    col_sums = jnp.sum(col_parts, axis=0)
    in_proj_grad, out_proj_grad = col_sums[0], col_sums[1]
    decay_grad = rate_chunks.reshape(rate_local.shape)
    slot_total = hidden_saved.shape[1]
    capacity = slot_total // (lax.axis_size("ctx") * lax.axis_size("exp"))
    buffer = slot_buffer(moe_grad, route, gate_prob, capacity)
    received_rows = lax.all_to_all(buffer, "exp", split_axis=0, concat_axis=1, tiled=True)
    all_rows = lax.all_gather(received_rows, "ctx", axis=1, tiled=True)
    weight_total = jnp.einsum(
        "lrf,lrd->lfd", hidden_saved, all_rows, preferred_element_type=jnp.float32
    )
    hidden_grad = jnp.einsum(
        "lrd,lfd->lrf", all_rows, w_down, preferred_element_type=jnp.float32
    ).astype(jnp.bfloat16)
    down_grad = weight_total.astype(jnp.bfloat16)
    return (input_grad, step_grad, in_proj_grad, out_proj_grad, decay_grad, down_grad, hidden_grad)


def solution(mesh):
    placed = (
        P("ctx", "exp"),
        P("ctx", "exp"),
        P(None, "exp"),
        P(None, "ctx"),
        P(None, "ctx"),
        P("exp"),
        P("ctx", None, "exp"),
        P(None, "exp"),
        P("ctx", "exp"),
        P(("ctx", "exp"), None),
        P(("ctx", "exp"), None),
        P(("ctx", "exp"), None),
        P("exp", "ctx", None),
        P("exp", None, "ctx"),
    )
    return jax.shard_map(
        body,
        mesh=mesh,
        in_specs=placed,
        out_specs=(
            P("ctx", "exp"),
            P("ctx", "exp"),
            P(None, "ctx"),
            P(None, "ctx"),
            P(None, "exp"),
            P("exp", "ctx", None),
            P("exp", None, "ctx"),
        ),
        check_vma=False,
    )
```

```python
import functools

import jax
import jax.numpy as jnp
from jax import lax
from jax.experimental import pallas as pl
from jax.experimental.pallas import tpu as pltpu
from jax.sharding import PartitionSpec as P

EXPERTS = 16


def local_scans_kernel(
    step_ref, inp_ref, grad_ref, bcol_ref, ccol_ref, rate_ref, first_ref,
    decay_ref, source_ref, states_ref, before_ref, seed_ref,
):
    count = step_ref.shape[0]

    def forward(t, state):
        stp, inp = step_ref[pl.ds(t, 1), :], inp_ref[pl.ds(t, 1), :]
        decay = jnp.exp(-stp * rate_ref[...])
        decay_ref[t] = decay
        source_ref[t] = ccol_ref[t] * grad_ref[pl.ds(t, 1), :]
        before_ref[t] = state
        state = decay * state + (stp * inp) * bcol_ref[t]
        states_ref[t] = state
        return state

    lax.fori_loop(0, count, forward, first_ref[...], unroll=8)

    def backward(i, running):
        t = count - 1 - i
        return decay_ref[t] * (source_ref[t] + running)

    seed_ref[...] = lax.fori_loop(0, count, backward, jnp.zeros_like(first_ref[...]), unroll=8)


def local_scans(steps, inputs, grads, bmats, cmats, rate, first_state):
    full = jax.ShapeDtypeStruct((steps.shape[0],) + rate.shape, jnp.float32)
    return pl.pallas_call(
        local_scans_kernel,
        out_shape=(full, full, full, full, jax.ShapeDtypeStruct(first_state.shape, jnp.float32)),
        cost_estimate=pl.CostEstimate(
            flops=8 * steps.shape[0] * rate.size,
            bytes_accessed=16 * steps.shape[0] * rate.size,
            transcendentals=steps.shape[0] * rate.size,
        ),
    )(steps, inputs, grads, bmats[:, :, None], cmats[:, :, None], rate, first_state)


def adjoint_scan_kernel(decay_ref, source_ref, entering_ref, adjoint_ref):
    count = decay_ref.shape[0]

    def backward(i, running):
        t = count - 1 - i
        value = source_ref[t] + running
        adjoint_ref[t] = value
        return decay_ref[t] * value

    lax.fori_loop(0, count, backward, entering_ref[...], unroll=8)


def adjoint_scan(decays, sources, entering):
    return pl.pallas_call(
        adjoint_scan_kernel,
        out_shape=jax.ShapeDtypeStruct(decays.shape, jnp.float32),
        cost_estimate=pl.CostEstimate(
            flops=2 * decays.size, bytes_accessed=12 * decays.size, transcendentals=0
        ),
    )(decays, sources, entering)


def relay_kernel(axis, count, pair_ref, out_ref, held, land, send_sems, recv_sems):
    me = lax.axis_index(axis)
    distances = []
    while 1 << len(distances) < count:
        distances.append(1 << len(distances))
    land[...] = jnp.zeros_like(land)
    barrier = pltpu.get_barrier_semaphore()
    expected = 0
    for d in distances:

        @pl.when(me >= d)
        def _():
            pl.semaphore_signal(barrier, 1, device_id={axis: me - d}, device_id_type=pl.DeviceIdType.MESH)

        @pl.when(me + d < count)
        def _():
            pl.semaphore_signal(barrier, 1, device_id={axis: me + d}, device_id_type=pl.DeviceIdType.MESH)

        expected = expected + (me >= d).astype(jnp.int32) + (me + d < count).astype(jnp.int32)
    pl.semaphore_wait(barrier, expected)
    rounds = distances + [1]
    for r, d in enumerate(rounds):
        last_round = r == len(rounds) - 1
        source = pair_ref if r == 0 else held.at[r - 1]
        copy = pltpu.make_async_remote_copy(
            src_ref=source,
            dst_ref=land.at[r],
            send_sem=send_sems.at[r],
            recv_sem=recv_sems.at[r],
            device_id={axis: lax.rem(me - d + count, count)},
            device_id_type=pl.DeviceIdType.MESH,
        )

        @pl.when(me >= d)
        def _():
            copy.start()

        if not last_round:
            held[r] = source[...]

        @pl.when(me + d < count)
        def _():
            copy.wait_recv()
            if not last_round:
                shrink, seed = source[0], source[1]
                held[r, 0] = shrink * land[r, 0]
                held[r, 1] = shrink * land[r, 1] + seed

        @pl.when(me >= d)
        def _():
            copy.wait_send()

    out_ref[...] = land[len(rounds) - 1, 1]


def relay(pair, axis, collective_id):
    count = lax.axis_size(axis)
    rounds = max(1, (count - 1).bit_length()) + 1
    return pl.pallas_call(
        functools.partial(relay_kernel, axis, count),
        out_shape=jax.ShapeDtypeStruct(pair.shape[1:], pair.dtype),
        scratch_shapes=[
            pltpu.VMEM((rounds - 1,) + pair.shape, pair.dtype),
            pltpu.VMEM((rounds,) + pair.shape, pair.dtype),
            pltpu.SemaphoreType.DMA((rounds,)),
            pltpu.SemaphoreType.DMA((rounds,)),
        ],
        compiler_params=pltpu.CompilerParams(collective_id=collective_id, has_side_effects=True),
    )(pair)


def reduce_kernel(cols_ref, parts_ref, cols_out, rate_out, cols_land, parts_land, chunk, chunk_land, sems):
    me_e, me_c = lax.axis_index("exp"), lax.axis_index("ctx")
    n_e, n_c = lax.axis_size("exp"), lax.axis_size("ctx")
    mesh_id = pl.DeviceIdType.MESH
    barrier = pltpu.get_barrier_semaphore()
    for k in range(1, n_e):
        pl.semaphore_signal(barrier, 1, device_id={"exp": lax.rem(me_e + k, n_e)}, device_id_type=mesh_id)
    for k in range(1, n_c):
        pl.semaphore_signal(barrier, 1, device_id={"ctx": lax.rem(me_c + k, n_c)}, device_id_type=mesh_id)
    pl.semaphore_wait(barrier, n_e - 1 + n_c - 1)

    def push(src, dst, axis, peer, slot):
        copy = pltpu.make_async_remote_copy(
            src_ref=src,
            dst_ref=dst,
            send_sem=sems.at[0, slot],
            recv_sem=sems.at[1, slot],
            device_id={axis: peer},
            device_id_type=mesh_id,
        )
        copy.start()
        return copy

    scattered = [
        push(parts_ref.at[lax.rem(me_c + k, n_c)], parts_land.at[me_c], "ctx", lax.rem(me_c + k, n_c), k)
        for k in range(1, n_c)
    ]
    gathered = [
        push(cols_ref, cols_land.at[me_e], "exp", lax.rem(me_e + k, n_e), 2 * n_c + k)
        for k in range(1, n_e)
    ]
    parts_land[me_c] = parts_ref[me_c]
    cols_land[me_e] = cols_ref[...]
    for copy in scattered:
        copy.wait()
    chunk[...] = jnp.sum(parts_land[...], axis=0)
    chunk_land[me_c] = chunk[...]
    spread = [
        push(chunk, chunk_land.at[me_c], "ctx", lax.rem(me_c + k, n_c), n_c + k)
        for k in range(1, n_c)
    ]
    for copy in gathered + spread:
        copy.wait()
    cols_out[...] = cols_land[...]
    rate_out[...] = chunk_land[...]


def reduce_partials(cols, parts, collective_id):
    n_e, n_c = lax.axis_size("exp"), lax.axis_size("ctx")
    return pl.pallas_call(
        reduce_kernel,
        out_shape=(
            jax.ShapeDtypeStruct((n_e,) + cols.shape, cols.dtype),
            jax.ShapeDtypeStruct(parts.shape, parts.dtype),
        ),
        scratch_shapes=[
            pltpu.VMEM((n_e,) + cols.shape, cols.dtype),
            pltpu.VMEM(parts.shape, parts.dtype),
            pltpu.VMEM(parts.shape[1:], parts.dtype),
            pltpu.VMEM(parts.shape, parts.dtype),
            pltpu.SemaphoreType.DMA((2, 2 * n_c + n_e)),
        ],
        compiler_params=pltpu.CompilerParams(collective_id=collective_id, has_side_effects=True),
    )(cols, parts)


def slot_buffer(moe_grad, route, gate_prob, capacity):
    pair_count = route.shape[0] * route.shape[1]
    weighted = (gate_prob[:, :, None] * moe_grad.astype(jnp.float32)[:, None, :]).astype(
        jnp.bfloat16
    )
    weighted = weighted.reshape(pair_count, moe_grad.shape[1])
    flat_route = route.reshape(pair_count)
    onehot = (flat_route[:, None] == jnp.arange(EXPERTS, dtype=jnp.int32)[None, :]).astype(
        jnp.int32
    )
    ranks = jnp.sum((jnp.cumsum(onehot, axis=0) - onehot) * onehot, axis=1)
    target = flat_route * capacity + ranks
    placing = (target[:, None] == jnp.arange(EXPERTS * capacity, dtype=jnp.int32)[None, :]).astype(
        jnp.bfloat16
    )
    buffer = jnp.einsum("ps,pd->sd", placing, weighted, preferred_element_type=jnp.float32).astype(
        jnp.bfloat16
    )
    return buffer.reshape(EXPERTS, capacity, moe_grad.shape[1])


def body(
    scan_input,
    step_size,
    decay_rate,
    input_proj,
    output_proj,
    skip_gain,
    block_states,
    end_grad,
    scan_grad,
    moe_grad,
    route,
    gate_prob,
    w_down,
    hidden_saved,
):
    inputs = scan_input.astype(jnp.float32)
    steps = step_size.astype(jnp.float32)
    grads = scan_grad.astype(jnp.float32)
    bmats = input_proj.T
    cmats = output_proj.T
    first_state = block_states[0]
    decays, sources, states, before, seed = local_scans(
        steps, inputs, grads, bmats, cmats, decay_rate, first_state
    )
    out_cols = jnp.sum(states * grads[:, None, :], axis=2)
    shrink = jnp.exp(-decay_rate * jnp.sum(steps, axis=0)[None])
    position = lax.axis_index("ctx")
    count = lax.axis_size("ctx")
    is_last = position == count - 1
    pair = jnp.stack(
        [jnp.where(is_last, 0.0, shrink), jnp.where(is_last, shrink * end_grad + seed, seed)]
    )
    entering = jnp.where(is_last, end_grad, relay(pair, "ctx", 4))
    adjoint = adjoint_scan(decays, sources, entering)
    input_grad = (
        steps * jnp.sum(bmats[:, :, None] * adjoint, axis=1) + skip_gain[None] * grads
    ).astype(jnp.bfloat16)
    step_grad = jnp.sum(
        adjoint * (bmats[:, :, None] * inputs[:, None, :] - decay_rate[None] * decays * before),
        axis=1,
    ).astype(jnp.bfloat16)
    in_cols = jnp.sum(adjoint * (steps * inputs)[:, None, :], axis=2)
    rate_local = jnp.sum(adjoint * (-steps[:, None, :] * decays * before), axis=0)
    ctx_count = lax.axis_size("ctx")
    rate_parts = rate_local.reshape(ctx_count, 1, rate_local.size // ctx_count)
    col_parts, rate_chunks = reduce_partials(jnp.stack([in_cols.T, out_cols.T]), rate_parts, 1)
    col_sums = jnp.sum(col_parts, axis=0)
    in_proj_grad, out_proj_grad = col_sums[0], col_sums[1]
    decay_grad = rate_chunks.reshape(rate_local.shape)
    slot_total = hidden_saved.shape[1]
    capacity = slot_total // (lax.axis_size("ctx") * lax.axis_size("exp"))
    buffer = slot_buffer(moe_grad, route, gate_prob, capacity)
    received_rows = lax.all_to_all(buffer, "exp", split_axis=0, concat_axis=1, tiled=True)
    all_rows = lax.all_gather(received_rows, "ctx", axis=1, tiled=True)
    weight_total = jnp.einsum(
        "lrf,lrd->lfd", hidden_saved, all_rows, preferred_element_type=jnp.float32
    )
    hidden_grad = jnp.einsum(
        "lrd,lfd->lrf", all_rows, w_down, preferred_element_type=jnp.float32
    ).astype(jnp.bfloat16)
    down_grad = weight_total.astype(jnp.bfloat16)
    return (input_grad, step_grad, in_proj_grad, out_proj_grad, decay_grad, down_grad, hidden_grad)


def solution(mesh):
    placed = (
        P("ctx", "exp"),
        P("ctx", "exp"),
        P(None, "exp"),
        P(None, "ctx"),
        P(None, "ctx"),
        P("exp"),
        P("ctx", None, "exp"),
        P(None, "exp"),
        P("ctx", "exp"),
        P(("ctx", "exp"), None),
        P(("ctx", "exp"), None),
        P(("ctx", "exp"), None),
        P("exp", "ctx", None),
        P("exp", None, "ctx"),
    )
    return jax.shard_map(
        body,
        mesh=mesh,
        in_specs=placed,
        out_specs=(
            P("ctx", "exp"),
            P("ctx", "exp"),
            P(None, "ctx"),
            P(None, "ctx"),
            P(None, "exp"),
            P("exp", "ctx", None),
            P("exp", None, "ctx"),
        ),
        check_vma=False,
    )
```

```python
import functools

import jax
import jax.numpy as jnp
from jax import lax
from jax.experimental import pallas as pl
from jax.experimental.pallas import tpu as pltpu
from jax.sharding import PartitionSpec as P

EXPERTS = 16


def local_scans_kernel(decay_ref, drive_ref, source_ref, first_ref, states_ref, before_ref, seed_ref):
    count = decay_ref.shape[0]

    def forward(t, state):
        before_ref[t] = state
        state = decay_ref[t] * state + drive_ref[t]
        states_ref[t] = state
        return state

    lax.fori_loop(0, count, forward, first_ref[...], unroll=8)

    def backward(i, running):
        t = count - 1 - i
        return decay_ref[t] * (source_ref[t] + running)

    seed_ref[...] = lax.fori_loop(0, count, backward, jnp.zeros_like(first_ref[...]), unroll=8)


def local_scans(decays, driving, sources, first_state):
    return pl.pallas_call(
        local_scans_kernel,
        out_shape=(
            jax.ShapeDtypeStruct(decays.shape, jnp.float32),
            jax.ShapeDtypeStruct(decays.shape, jnp.float32),
            jax.ShapeDtypeStruct(first_state.shape, jnp.float32),
        ),
        cost_estimate=pl.CostEstimate(
            flops=4 * decays.size, bytes_accessed=20 * decays.size, transcendentals=0
        ),
    )(decays, driving, sources, first_state)


def adjoint_scan_kernel(decay_ref, source_ref, entering_ref, adjoint_ref):
    count = decay_ref.shape[0]

    def backward(i, running):
        t = count - 1 - i
        value = source_ref[t] + running
        adjoint_ref[t] = value
        return decay_ref[t] * value

    lax.fori_loop(0, count, backward, entering_ref[...], unroll=8)


def adjoint_scan(decays, sources, entering):
    return pl.pallas_call(
        adjoint_scan_kernel,
        out_shape=jax.ShapeDtypeStruct(decays.shape, jnp.float32),
        cost_estimate=pl.CostEstimate(
            flops=2 * decays.size, bytes_accessed=12 * decays.size, transcendentals=0
        ),
    )(decays, sources, entering)


def weight_grad_kernel(saved_ref, rows_ref, out_ref):
    out_ref[...] = jnp.dot(
        saved_ref[...], rows_ref[...], preferred_element_type=jnp.float32
    ).astype(out_ref.dtype)


def weight_grad(saved_t, rows, tile=512):
    features, slots = saved_t.shape
    width = rows.shape[1]
    return pl.pallas_call(
        weight_grad_kernel,
        out_shape=jax.ShapeDtypeStruct((features, width), jnp.bfloat16),
        grid=(width // tile,),
        in_specs=[
            pl.BlockSpec((features, slots), lambda j: (0, 0)),
            pl.BlockSpec((slots, tile), lambda j: (0, j)),
        ],
        out_specs=pl.BlockSpec((features, tile), lambda j: (0, j)),
        cost_estimate=pl.CostEstimate(
            flops=2 * features * slots * width,
            bytes_accessed=2 * (features * slots + slots * width + features * width),
            transcendentals=0,
        ),
    )(saved_t, rows)


def relay_kernel(axis, count, pair_ref, out_ref, held, land, send_sems, recv_sems):
    me = lax.axis_index(axis)
    distances = []
    while 1 << len(distances) < count:
        distances.append(1 << len(distances))
    land[...] = jnp.zeros_like(land)
    barrier = pltpu.get_barrier_semaphore()
    expected = 0
    for d in distances:

        @pl.when(me >= d)
        def _():
            pl.semaphore_signal(barrier, 1, device_id={axis: me - d}, device_id_type=pl.DeviceIdType.MESH)

        @pl.when(me + d < count)
        def _():
            pl.semaphore_signal(barrier, 1, device_id={axis: me + d}, device_id_type=pl.DeviceIdType.MESH)

        expected = expected + (me >= d).astype(jnp.int32) + (me + d < count).astype(jnp.int32)
    pl.semaphore_wait(barrier, expected)
    rounds = distances + [1]
    for r, d in enumerate(rounds):
        last_round = r == len(rounds) - 1
        source = pair_ref if r == 0 else held.at[r - 1]
        copy = pltpu.make_async_remote_copy(
            src_ref=source,
            dst_ref=land.at[r],
            send_sem=send_sems.at[r],
            recv_sem=recv_sems.at[r],
            device_id={axis: lax.rem(me - d + count, count)},
            device_id_type=pl.DeviceIdType.MESH,
        )

        @pl.when(me >= d)
        def _():
            copy.start()

        if not last_round:
            held[r] = source[...]

        @pl.when(me + d < count)
        def _():
            copy.wait_recv()
            if not last_round:
                shrink, seed = source[0], source[1]
                held[r, 0] = shrink * land[r, 0]
                held[r, 1] = shrink * land[r, 1] + seed

        @pl.when(me >= d)
        def _():
            copy.wait_send()

    out_ref[...] = land[len(rounds) - 1, 1]


def relay(pair, axis, collective_id):
    count = lax.axis_size(axis)
    rounds = max(1, (count - 1).bit_length()) + 1
    return pl.pallas_call(
        functools.partial(relay_kernel, axis, count),
        out_shape=jax.ShapeDtypeStruct(pair.shape[1:], pair.dtype),
        scratch_shapes=[
            pltpu.VMEM((rounds - 1,) + pair.shape, pair.dtype),
            pltpu.VMEM((rounds,) + pair.shape, pair.dtype),
            pltpu.SemaphoreType.DMA((rounds,)),
            pltpu.SemaphoreType.DMA((rounds,)),
        ],
        compiler_params=pltpu.CompilerParams(collective_id=collective_id, has_side_effects=True),
    )(pair)


def reduce_kernel(cols_ref, parts_ref, cols_out, rate_out, cols_land, parts_land, chunk, chunk_land, sems):
    me_e, me_c = lax.axis_index("exp"), lax.axis_index("ctx")
    n_e, n_c = lax.axis_size("exp"), lax.axis_size("ctx")
    mesh_id = pl.DeviceIdType.MESH
    barrier = pltpu.get_barrier_semaphore()
    for k in range(1, n_e):
        pl.semaphore_signal(barrier, 1, device_id={"exp": lax.rem(me_e + k, n_e)}, device_id_type=mesh_id)
    for k in range(1, n_c):
        pl.semaphore_signal(barrier, 1, device_id={"ctx": lax.rem(me_c + k, n_c)}, device_id_type=mesh_id)
    pl.semaphore_wait(barrier, n_e - 1 + n_c - 1)

    def push(src, dst, axis, peer, slot):
        copy = pltpu.make_async_remote_copy(
            src_ref=src,
            dst_ref=dst,
            send_sem=sems.at[0, slot],
            recv_sem=sems.at[1, slot],
            device_id={axis: peer},
            device_id_type=mesh_id,
        )
        copy.start()
        return copy

    scattered = [
        push(parts_ref.at[lax.rem(me_c + k, n_c)], parts_land.at[me_c], "ctx", lax.rem(me_c + k, n_c), k)
        for k in range(1, n_c)
    ]
    gathered = [
        push(cols_ref, cols_land.at[me_e], "exp", lax.rem(me_e + k, n_e), 2 * n_c + k)
        for k in range(1, n_e)
    ]
    parts_land[me_c] = parts_ref[me_c]
    cols_land[me_e] = cols_ref[...]
    for copy in scattered:
        copy.wait()
    chunk[...] = jnp.sum(parts_land[...], axis=0)
    chunk_land[me_c] = chunk[...]
    spread = [
        push(chunk, chunk_land.at[me_c], "ctx", lax.rem(me_c + k, n_c), n_c + k)
        for k in range(1, n_c)
    ]
    for copy in gathered + spread:
        copy.wait()
    cols_out[...] = cols_land[...]
    rate_out[...] = chunk_land[...]


def reduce_partials(cols, parts, collective_id):
    n_e, n_c = lax.axis_size("exp"), lax.axis_size("ctx")
    return pl.pallas_call(
        reduce_kernel,
        out_shape=(
            jax.ShapeDtypeStruct((n_e,) + cols.shape, cols.dtype),
            jax.ShapeDtypeStruct(parts.shape, parts.dtype),
        ),
        scratch_shapes=[
            pltpu.VMEM((n_e,) + cols.shape, cols.dtype),
            pltpu.VMEM(parts.shape, parts.dtype),
            pltpu.VMEM(parts.shape[1:], parts.dtype),
            pltpu.VMEM(parts.shape, parts.dtype),
            pltpu.SemaphoreType.DMA((2, 2 * n_c + n_e)),
        ],
        compiler_params=pltpu.CompilerParams(collective_id=collective_id, has_side_effects=True),
    )(cols, parts)


def slot_buffer(moe_grad, route, gate_prob, capacity):
    pair_count = route.shape[0] * route.shape[1]
    weighted = (gate_prob[:, :, None] * moe_grad.astype(jnp.float32)[:, None, :]).astype(
        jnp.bfloat16
    )
    weighted = weighted.reshape(pair_count, moe_grad.shape[1])
    flat_route = route.reshape(pair_count)
    onehot = (flat_route[:, None] == jnp.arange(EXPERTS, dtype=jnp.int32)[None, :]).astype(
        jnp.int32
    )
    ranks = jnp.sum((jnp.cumsum(onehot, axis=0) - onehot) * onehot, axis=1)
    target = flat_route * capacity + ranks
    placing = (target[:, None] == jnp.arange(EXPERTS * capacity, dtype=jnp.int32)[None, :]).astype(
        jnp.bfloat16
    )
    buffer = jnp.einsum("ps,pd->sd", placing, weighted, preferred_element_type=jnp.float32).astype(
        jnp.bfloat16
    )
    return buffer.reshape(EXPERTS, capacity, moe_grad.shape[1])


def body(
    scan_input,
    step_size,
    decay_rate,
    input_proj,
    output_proj,
    skip_gain,
    block_states,
    end_grad,
    scan_grad,
    moe_grad,
    route,
    gate_prob,
    w_down,
    hidden_saved,
):
    inputs = scan_input.astype(jnp.float32)
    steps = step_size.astype(jnp.float32)
    grads = scan_grad.astype(jnp.float32)
    bmats = input_proj.T
    cmats = output_proj.T
    first_state = block_states[0]
    decays = jnp.exp(-steps[:, None, :] * decay_rate[None])
    driving = (steps * inputs)[:, None, :] * bmats[:, :, None]
    sources = cmats[:, :, None] * grads[:, None, :]
    states, before, seed = local_scans(decays, driving, sources, first_state)
    out_cols = jnp.sum(states * grads[:, None, :], axis=2)
    shrink = jnp.exp(-decay_rate * jnp.sum(steps, axis=0)[None])
    position = lax.axis_index("ctx")
    count = lax.axis_size("ctx")
    is_last = position == count - 1
    pair = jnp.stack(
        [jnp.where(is_last, 0.0, shrink), jnp.where(is_last, shrink * end_grad + seed, seed)]
    )
    entering = jnp.where(is_last, end_grad, relay(pair, "ctx", 4))
    adjoint = adjoint_scan(decays, sources, entering)
    input_grad = (
        steps * jnp.sum(bmats[:, :, None] * adjoint, axis=1) + skip_gain[None] * grads
    ).astype(jnp.bfloat16)
    step_grad = jnp.sum(
        adjoint * (bmats[:, :, None] * inputs[:, None, :] - decay_rate[None] * decays * before),
        axis=1,
    ).astype(jnp.bfloat16)
    in_cols = jnp.sum(adjoint * (steps * inputs)[:, None, :], axis=2)
    rate_local = jnp.sum(adjoint * (-steps[:, None, :] * decays * before), axis=0)
    ctx_count = lax.axis_size("ctx")
    rate_parts = rate_local.reshape(ctx_count, 1, rate_local.size // ctx_count)
    col_parts, rate_chunks = reduce_partials(jnp.stack([in_cols.T, out_cols.T]), rate_parts, 1)
    col_sums = jnp.sum(col_parts, axis=0)
    in_proj_grad, out_proj_grad = col_sums[0], col_sums[1]
    decay_grad = rate_chunks.reshape(rate_local.shape)
    slot_total = hidden_saved.shape[1]
    capacity = slot_total // (lax.axis_size("ctx") * lax.axis_size("exp"))
    buffer = slot_buffer(moe_grad, route, gate_prob, capacity)
    received_rows = lax.all_to_all(buffer, "exp", split_axis=0, concat_axis=1, tiled=True)
    all_rows = lax.all_gather(received_rows, "ctx", axis=1, tiled=True)
    down_grad = weight_grad(hidden_saved[0].T, all_rows[0])[None]
    hidden_grad = jnp.einsum(
        "lrd,lfd->lrf", all_rows, w_down, preferred_element_type=jnp.float32
    ).astype(jnp.bfloat16)
    return (input_grad, step_grad, in_proj_grad, out_proj_grad, decay_grad, down_grad, hidden_grad)


def solution(mesh):
    placed = (
        P("ctx", "exp"),
        P("ctx", "exp"),
        P(None, "exp"),
        P(None, "ctx"),
        P(None, "ctx"),
        P("exp"),
        P("ctx", None, "exp"),
        P(None, "exp"),
        P("ctx", "exp"),
        P(("ctx", "exp"), None),
        P(("ctx", "exp"), None),
        P(("ctx", "exp"), None),
        P("exp", "ctx", None),
        P("exp", None, "ctx"),
    )
    return jax.shard_map(
        body,
        mesh=mesh,
        in_specs=placed,
        out_specs=(
            P("ctx", "exp"),
            P("ctx", "exp"),
            P(None, "ctx"),
            P(None, "ctx"),
            P(None, "exp"),
            P("exp", "ctx", None),
            P("exp", None, "ctx"),
        ),
        check_vma=False,
    )
```

```python
import functools

import jax
import jax.numpy as jnp
from jax import lax
from jax.experimental import pallas as pl
from jax.experimental.pallas import tpu as pltpu
from jax.sharding import PartitionSpec as P

EXPERTS = 16


def local_scans_kernel(decay_ref, drive_ref, source_ref, first_ref, states_ref, before_ref, seed_ref):
    count = decay_ref.shape[0]

    def forward(t, state):
        before_ref[t] = state
        state = decay_ref[t] * state + drive_ref[t]
        states_ref[t] = state
        return state

    lax.fori_loop(0, count, forward, first_ref[...], unroll=16)

    def backward(i, running):
        t = count - 1 - i
        return decay_ref[t] * (source_ref[t] + running)

    seed_ref[...] = lax.fori_loop(0, count, backward, jnp.zeros_like(first_ref[...]), unroll=16)


def local_scans(decays, driving, sources, first_state):
    return pl.pallas_call(
        local_scans_kernel,
        out_shape=(
            jax.ShapeDtypeStruct(decays.shape, jnp.float32),
            jax.ShapeDtypeStruct(decays.shape, jnp.float32),
            jax.ShapeDtypeStruct(first_state.shape, jnp.float32),
        ),
        cost_estimate=pl.CostEstimate(
            flops=4 * decays.size, bytes_accessed=20 * decays.size, transcendentals=0
        ),
    )(decays, driving, sources, first_state)


def adjoint_scan_kernel(decay_ref, source_ref, entering_ref, adjoint_ref):
    count = decay_ref.shape[0]

    def backward(i, running):
        t = count - 1 - i
        value = source_ref[t] + running
        adjoint_ref[t] = value
        return decay_ref[t] * value

    lax.fori_loop(0, count, backward, entering_ref[...], unroll=16)


def adjoint_scan(decays, sources, entering):
    return pl.pallas_call(
        adjoint_scan_kernel,
        out_shape=jax.ShapeDtypeStruct(decays.shape, jnp.float32),
        cost_estimate=pl.CostEstimate(
            flops=2 * decays.size, bytes_accessed=12 * decays.size, transcendentals=0
        ),
    )(decays, sources, entering)


def relay_kernel(axis, count, pair_ref, out_ref, held, land, send_sems, recv_sems):
    me = lax.axis_index(axis)
    distances = []
    while 1 << len(distances) < count:
        distances.append(1 << len(distances))
    land[...] = jnp.zeros_like(land)
    barrier = pltpu.get_barrier_semaphore()
    expected = 0
    for d in distances:

        @pl.when(me >= d)
        def _():
            pl.semaphore_signal(barrier, 1, device_id={axis: me - d}, device_id_type=pl.DeviceIdType.MESH)

        @pl.when(me + d < count)
        def _():
            pl.semaphore_signal(barrier, 1, device_id={axis: me + d}, device_id_type=pl.DeviceIdType.MESH)

        expected = expected + (me >= d).astype(jnp.int32) + (me + d < count).astype(jnp.int32)
    pl.semaphore_wait(barrier, expected)
    rounds = distances + [1]
    for r, d in enumerate(rounds):
        last_round = r == len(rounds) - 1
        source = pair_ref if r == 0 else held.at[r - 1]
        copy = pltpu.make_async_remote_copy(
            src_ref=source,
            dst_ref=land.at[r],
            send_sem=send_sems.at[r],
            recv_sem=recv_sems.at[r],
            device_id={axis: lax.rem(me - d + count, count)},
            device_id_type=pl.DeviceIdType.MESH,
        )

        @pl.when(me >= d)
        def _():
            copy.start()

        if not last_round:
            held[r] = source[...]

        @pl.when(me + d < count)
        def _():
            copy.wait_recv()
            if not last_round:
                shrink, seed = source[0], source[1]
                held[r, 0] = shrink * land[r, 0]
                held[r, 1] = shrink * land[r, 1] + seed

        @pl.when(me >= d)
        def _():
            copy.wait_send()

    out_ref[...] = land[len(rounds) - 1, 1]


def relay(pair, axis, collective_id):
    count = lax.axis_size(axis)
    rounds = max(1, (count - 1).bit_length()) + 1
    return pl.pallas_call(
        functools.partial(relay_kernel, axis, count),
        out_shape=jax.ShapeDtypeStruct(pair.shape[1:], pair.dtype),
        scratch_shapes=[
            pltpu.VMEM((rounds - 1,) + pair.shape, pair.dtype),
            pltpu.VMEM((rounds,) + pair.shape, pair.dtype),
            pltpu.SemaphoreType.DMA((rounds,)),
            pltpu.SemaphoreType.DMA((rounds,)),
        ],
        compiler_params=pltpu.CompilerParams(collective_id=collective_id, has_side_effects=True),
    )(pair)


def reduce_kernel(cols_ref, parts_ref, cols_out, rate_out, cols_land, parts_land, chunk, chunk_land, sems):
    me_e, me_c = lax.axis_index("exp"), lax.axis_index("ctx")
    n_e, n_c = lax.axis_size("exp"), lax.axis_size("ctx")
    mesh_id = pl.DeviceIdType.MESH
    barrier = pltpu.get_barrier_semaphore()
    for k in range(1, n_e):
        pl.semaphore_signal(barrier, 1, device_id={"exp": lax.rem(me_e + k, n_e)}, device_id_type=mesh_id)
    for k in range(1, n_c):
        pl.semaphore_signal(barrier, 1, device_id={"ctx": lax.rem(me_c + k, n_c)}, device_id_type=mesh_id)
    pl.semaphore_wait(barrier, n_e - 1 + n_c - 1)

    def push(src, dst, axis, peer, slot):
        copy = pltpu.make_async_remote_copy(
            src_ref=src,
            dst_ref=dst,
            send_sem=sems.at[0, slot],
            recv_sem=sems.at[1, slot],
            device_id={axis: peer},
            device_id_type=mesh_id,
        )
        copy.start()
        return copy

    scattered = [
        push(parts_ref.at[lax.rem(me_c + k, n_c)], parts_land.at[me_c], "ctx", lax.rem(me_c + k, n_c), k)
        for k in range(1, n_c)
    ]
    gathered = [
        push(cols_ref, cols_land.at[me_e], "exp", lax.rem(me_e + k, n_e), 2 * n_c + k)
        for k in range(1, n_e)
    ]
    parts_land[me_c] = parts_ref[me_c]
    cols_land[me_e] = cols_ref[...]
    for copy in scattered:
        copy.wait()
    chunk[...] = jnp.sum(parts_land[...], axis=0)
    chunk_land[me_c] = chunk[...]
    spread = [
        push(chunk, chunk_land.at[me_c], "ctx", lax.rem(me_c + k, n_c), n_c + k)
        for k in range(1, n_c)
    ]
    for copy in gathered + spread:
        copy.wait()
    cols_out[...] = cols_land[...]
    rate_out[...] = chunk_land[...]


def reduce_partials(cols, parts, collective_id):
    n_e, n_c = lax.axis_size("exp"), lax.axis_size("ctx")
    return pl.pallas_call(
        reduce_kernel,
        out_shape=(
            jax.ShapeDtypeStruct((n_e,) + cols.shape, cols.dtype),
            jax.ShapeDtypeStruct(parts.shape, parts.dtype),
        ),
        scratch_shapes=[
            pltpu.VMEM((n_e,) + cols.shape, cols.dtype),
            pltpu.VMEM(parts.shape, parts.dtype),
            pltpu.VMEM(parts.shape[1:], parts.dtype),
            pltpu.VMEM(parts.shape, parts.dtype),
            pltpu.SemaphoreType.DMA((2, 2 * n_c + n_e)),
        ],
        compiler_params=pltpu.CompilerParams(collective_id=collective_id, has_side_effects=True),
    )(cols, parts)


def slot_buffer(moe_grad, route, gate_prob, capacity):
    pair_count = route.shape[0] * route.shape[1]
    weighted = (gate_prob[:, :, None] * moe_grad.astype(jnp.float32)[:, None, :]).astype(
        jnp.bfloat16
    )
    weighted = weighted.reshape(pair_count, moe_grad.shape[1])
    flat_route = route.reshape(pair_count)
    onehot = (flat_route[:, None] == jnp.arange(EXPERTS, dtype=jnp.int32)[None, :]).astype(
        jnp.int32
    )
    ranks = jnp.sum((jnp.cumsum(onehot, axis=0) - onehot) * onehot, axis=1)
    target = flat_route * capacity + ranks
    placing = (target[:, None] == jnp.arange(EXPERTS * capacity, dtype=jnp.int32)[None, :]).astype(
        jnp.bfloat16
    )
    buffer = jnp.einsum("ps,pd->sd", placing, weighted, preferred_element_type=jnp.float32).astype(
        jnp.bfloat16
    )
    return buffer.reshape(EXPERTS, capacity, moe_grad.shape[1])


def body(
    scan_input,
    step_size,
    decay_rate,
    input_proj,
    output_proj,
    skip_gain,
    block_states,
    end_grad,
    scan_grad,
    moe_grad,
    route,
    gate_prob,
    w_down,
    hidden_saved,
):
    inputs = scan_input.astype(jnp.float32)
    steps = step_size.astype(jnp.float32)
    grads = scan_grad.astype(jnp.float32)
    bmats = input_proj.T
    cmats = output_proj.T
    first_state = block_states[0]
    decays = jnp.exp(-steps[:, None, :] * decay_rate[None])
    driving = (steps * inputs)[:, None, :] * bmats[:, :, None]
    sources = cmats[:, :, None] * grads[:, None, :]
    states, before, seed = local_scans(decays, driving, sources, first_state)
    out_cols = jnp.sum(states * grads[:, None, :], axis=2)
    shrink = jnp.exp(-decay_rate * jnp.sum(steps, axis=0)[None])
    position = lax.axis_index("ctx")
    count = lax.axis_size("ctx")
    is_last = position == count - 1
    pair = jnp.stack(
        [jnp.where(is_last, 0.0, shrink), jnp.where(is_last, shrink * end_grad + seed, seed)]
    )
    entering = jnp.where(is_last, end_grad, relay(pair, "ctx", 4))
    adjoint = adjoint_scan(decays, sources, entering)
    input_grad = (
        steps * jnp.sum(bmats[:, :, None] * adjoint, axis=1) + skip_gain[None] * grads
    ).astype(jnp.bfloat16)
    step_grad = jnp.sum(
        adjoint * (bmats[:, :, None] * inputs[:, None, :] - decay_rate[None] * decays * before),
        axis=1,
    ).astype(jnp.bfloat16)
    in_cols = jnp.sum(adjoint * (steps * inputs)[:, None, :], axis=2)
    rate_local = jnp.sum(adjoint * (-steps[:, None, :] * decays * before), axis=0)
    ctx_count = lax.axis_size("ctx")
    rate_parts = rate_local.reshape(ctx_count, 1, rate_local.size // ctx_count)
    col_parts, rate_chunks = reduce_partials(jnp.stack([in_cols.T, out_cols.T]), rate_parts, 1)
    col_sums = jnp.sum(col_parts, axis=0)
    in_proj_grad, out_proj_grad = col_sums[0], col_sums[1]
    decay_grad = rate_chunks.reshape(rate_local.shape)
    slot_total = hidden_saved.shape[1]
    capacity = slot_total // (lax.axis_size("ctx") * lax.axis_size("exp"))
    buffer = slot_buffer(moe_grad, route, gate_prob, capacity)
    received_rows = lax.all_to_all(buffer, "exp", split_axis=0, concat_axis=1, tiled=True)
    all_rows = lax.all_gather(received_rows, "ctx", axis=1, tiled=True)
    weight_total = jnp.einsum(
        "lrf,lrd->lfd", hidden_saved, all_rows, preferred_element_type=jnp.float32
    )
    hidden_grad = jnp.einsum(
        "lrd,lfd->lrf", all_rows, w_down, preferred_element_type=jnp.float32
    ).astype(jnp.bfloat16)
    down_grad = weight_total.astype(jnp.bfloat16)
    return (input_grad, step_grad, in_proj_grad, out_proj_grad, decay_grad, down_grad, hidden_grad)


def solution(mesh):
    placed = (
        P("ctx", "exp"),
        P("ctx", "exp"),
        P(None, "exp"),
        P(None, "ctx"),
        P(None, "ctx"),
        P("exp"),
        P("ctx", None, "exp"),
        P(None, "exp"),
        P("ctx", "exp"),
        P(("ctx", "exp"), None),
        P(("ctx", "exp"), None),
        P(("ctx", "exp"), None),
        P("exp", "ctx", None),
        P("exp", None, "ctx"),
    )
    return jax.shard_map(
        body,
        mesh=mesh,
        in_specs=placed,
        out_specs=(
            P("ctx", "exp"),
            P("ctx", "exp"),
            P(None, "ctx"),
            P(None, "ctx"),
            P(None, "exp"),
            P("exp", "ctx", None),
            P("exp", None, "ctx"),
        ),
        check_vma=False,
    )
```
